32 devices in a mesh: head: 2 (over y), view: 4 (over z), row: 4 (over x, core).
Axes of the slice: x: 2, y: 2, z: 4, core: 2. Of those that a mesh axis runs over, the one named last changes fastest.
Arguments:
- query_feats: bfloat16 [4, 32, 16, 1024], P('view', 'row', None, 'head'), may hold values from -125 to 125
- key_feats: bfloat16 [4, 32, 16, 1024], P('view', 'row', None, 'head'), may hold values from -7 to 7
- value_feats: bfloat16 [4, 32, 16, 1024], P('view', 'row', None, 'head'), may hold values from -6 to 6
- target: bfloat16 [4, 32, 16, 1024], P('view', 'row', None, 'head'), may hold values from -6 to 6
- token_rates: float32 [4, 2, 512], P('view', 'head', 'row'), may hold values from 5 to 100
- row_reach: int32 [32], P('row'), may hold values from 1 to 2
- view_counts: int32 [4], P('view'), may hold values from 170 to 512
- w_first: bfloat16 [2, 512, 512], P('head'), may hold values from -0.25 to 0.25
- w_third: bfloat16 [2, 512, 512], P('head'), may hold values from -0.25 to 0.25
- w_second: bfloat16 [2, 512, 512], P('head'), may hold values from -0.25 to 0.25
Outputs:
- fast_out: bfloat16 [4, 32, 16, 1024], P('view', 'row', None, 'head')
The draws below stay inside these ranges and needn't reach their ends.
All inputs are finite; a program needn't handle non-finite values.
Results may differ from the reference program's by a relative error of at most 0.03.
Values may be sent and summed in bfloat16 or wider, within the bound.
A program may use at most 64 MiB of HBM per device.

```python
import math
import jax
import jax.numpy as jnp
from jax import lax

HEADS = 2
HD = 512
ATT_HD = 128
COLS = 16
ROWS_DEV = 8
HALO = 2
NR = 32
VIEWS = 4
VIEW_TOK = 512


def draw_pair(key):
    grid_shape = (VIEWS, NR, COLS, HEADS * HD)
    keys_draw = jax.random.truncated_normal(jax.random.fold_in(key, 11), -6.0, 6.0, grid_shape, jnp.float32)
    query_draw = jax.random.truncated_normal(jax.random.fold_in(key, 12), -6.0, 6.0, grid_shape, jnp.float32)
    return (query_draw, keys_draw)


def draw_query_feats(key, part):
    return draw_pair(key)[0].astype(jnp.bfloat16)


def draw_key_feats(key, part):
    return draw_pair(key)[1].astype(jnp.bfloat16)


def draw_view_counts(key, part):
    position = jnp.arange(VIEWS, dtype=jnp.int32)
    lowest = VIEW_TOK // 3
    growth = (VIEW_TOK - lowest - VIEW_TOK // 8) * position // max(VIEWS - 1, 1)
    jitter = jax.random.randint(key, (VIEWS,), 0, VIEW_TOK // 8 + 1, jnp.int32)
    return jnp.minimum(lowest + growth + jitter, VIEW_TOK).astype(jnp.int32)


def plant(values, stream_key, low, high):
    spot = [jax.random.randint(jax.random.fold_in(stream_key, axis), (), 0, length) for axis, length in enumerate(values.shape)]
    widest = values.shape.index(max(values.shape))
    beside = spot[:widest] + [(spot[widest] + 1) % values.shape[widest]] + spot[widest + 1:]
    return values.at[tuple(spot)].set(low).at[tuple(beside)].set(high)


def block_levels(rng, dims, split, low, top_value):
    loudness, own = 1.0, jax.random.fold_in(rng, 6)
    for dim, shards_of in split:
        draws = jnp.exp(jax.random.uniform(jax.random.fold_in(own, dim), (shards_of,), jnp.float32, low / len(split), top_value / len(split)))
        loudness = loudness * jnp.repeat(draws, dims[dim] // shards_of).reshape([-1 if axis == dim else 1 for axis in range(len(dims))])
    return loudness


def noise(rng, dims, scale, reach, split=(), held_as=jnp.bfloat16):
    entries = scale * jax.random.normal(rng, dims, jnp.float32)
    if split:
        entries = entries * block_levels(rng, dims, split, -0.22, 0.18)
    return jnp.clip(entries, -reach, reach).astype(held_as)


def setup_inputs(seed: int = 0) -> dict:
    splits = jax.random.split(jax.random.key(seed), 11)
    return {
        "query_feats": draw_query_feats(jax.random.fold_in(splits[10], 71), 0),
        "key_feats": draw_key_feats(jax.random.fold_in(splits[10], 71), 0),
        "value_feats": noise(splits[2], (VIEWS, NR, COLS, HEADS * HD), 1.0, 6.0, ((0, 4), (1, 4), (3, 2))),
        "target": noise(splits[3], (VIEWS, NR, COLS, HEADS * HD), 1.0, 6.0, ((0, 4), (1, 4), (3, 2))),
        "token_rates": jnp.clip(jnp.exp(math.log(100.0) - 2.9957323 * jax.random.uniform(splits[4], (VIEWS, HEADS, NR * COLS), jnp.float32) ** block_levels(splits[4], (VIEWS, HEADS, NR * COLS), ((0, 4), (1, 2), (2, 4)), -0.2, 0.2)), 5.0, 100.0),
        "row_reach": plant(jax.random.randint(splits[5], (NR,), 1, 3), jax.random.fold_in(splits[5], 1), 1, 2).astype(jnp.int32),
        "view_counts": draw_view_counts(jax.random.fold_in(splits[10], 71), 0),
        "w_first": noise(splits[7], (HEADS, HD, HD), HD ** -0.5, 0.25, ((0, 2),)),
        "w_third": noise(splits[8], (HEADS, HD, HD), HD ** -0.5, 0.25, ((0, 2),)),
        "w_second": noise(splits[9], (HEADS, HD, HD), HD ** -0.5, 0.25, ((0, 2),)),
    }


def silu_slope(values_in):
    sigmoid_x = jax.nn.sigmoid(values_in)
    return sigmoid_x * (1.0 + values_in * (1.0 - sigmoid_x))

def attend(query_rows, key_rows, value_rows, q_row_ids, k_row_ids, q_tok, k_tok, k_valid, q_reach, grid_rows):
    count_q = query_rows.shape[0]
    count_k = key_rows.shape[0]
    groups = query_rows.shape[1] // ATT_HD
    query_heads = query_rows.reshape(count_q, groups, ATT_HD).astype(jnp.float32)
    key_heads = key_rows.reshape(count_k, groups, ATT_HD).astype(jnp.float32)
    value_heads = value_rows.reshape(count_k, groups, ATT_HD).astype(jnp.float32)
    scores = jnp.einsum('qhd,khd->hqk', query_heads, key_heads) / math.sqrt(ATT_HD)
    inside = (k_row_ids >= 0) & (k_row_ids < grid_rows)
    in_band = jnp.abs(k_row_ids[None, :] - q_row_ids[:, None]) <= q_reach[:, None]
    allowed = in_band & inside[None, :] & (k_valid[None, :] | (k_tok[None, :] == q_tok[:, None]))
    scores = jnp.where(allowed[None], scores, -1e+30)
    row_top = lax.optimization_barrier(jnp.max(scores, -1, keepdims=True))
    powers = jnp.exp(scores - row_top)
    weights = (powers / lax.optimization_barrier(jnp.sum(powers, -1, keepdims=True))).astype(jnp.bfloat16)
    output_rows = jnp.einsum('hqk,khd->qhd', weights.astype(jnp.float32), value_heads)
    return output_rows.reshape(count_q, groups * ATT_HD).astype(jnp.bfloat16)

def renorm(old_matrix, grad, total_valid):
    old_rows = old_matrix.astype(jnp.float32)
    raised = old_rows + grad / total_valid
    rescale = jnp.sqrt(lax.optimization_barrier(jnp.sum(old_rows * old_rows, -1, keepdims=True)) + 1e-06) / jnp.sqrt(lax.optimization_barrier(jnp.sum(raised * raised, -1, keepdims=True)) + 1e-06)
    return (raised * rescale).astype(jnp.bfloat16)

def reference(query_feats, key_feats, value_feats, target, token_rates, row_reach, view_counts, w_first, w_third, w_second):
    feat_width = HEADS * HD
    row_pad = ((0, 0), (HALO, HALO), (0, 0), (0, 0))
    key_pad = jnp.pad(key_feats, row_pad)
    value_pad = jnp.pad(value_feats, row_pad)
    blocks = NR // ROWS_DEV
    key_span = ROWS_DEV + 2 * HALO

    def attend_block(flat_index):
        view_index = (flat_index // blocks).astype(jnp.int32)
        row_start = (flat_index % blocks * ROWS_DEV).astype(jnp.int32)
        zero_index = jnp.zeros((), jnp.int32)
        q_blk = lax.dynamic_slice(query_feats, (view_index, row_start, zero_index, zero_index), (1, ROWS_DEV, COLS, feat_width))[0].reshape(ROWS_DEV * COLS, feat_width)
        k_blk = lax.dynamic_slice(key_pad, (view_index, row_start, zero_index, zero_index), (1, key_span, COLS, feat_width))[0].reshape(key_span * COLS, feat_width)
        v_blk = lax.dynamic_slice(value_pad, (view_index, row_start, zero_index, zero_index), (1, key_span, COLS, feat_width))[0].reshape(key_span * COLS, feat_width)
        q_row_ids = row_start + jnp.repeat(jnp.arange(ROWS_DEV, dtype=jnp.int32), COLS)
        k_row_ids = row_start - HALO + jnp.repeat(jnp.arange(key_span, dtype=jnp.int32), COLS)
        q_tok = q_row_ids * COLS + jnp.tile(jnp.arange(COLS, dtype=jnp.int32), ROWS_DEV)
        k_tok = k_row_ids * COLS + jnp.tile(jnp.arange(COLS, dtype=jnp.int32), key_span)
        view_total = view_counts[view_index]
        k_valid = k_tok < view_total
        q_reach = row_reach[q_row_ids]
        return attend(q_blk, k_blk, v_blk, q_row_ids, k_row_ids, q_tok, k_tok, k_valid, q_reach, NR)
    blocks_out = lax.map(attend_block, jnp.arange(VIEWS * blocks, dtype=jnp.int32))
    total_tok = VIEWS * NR * COLS
    attended = blocks_out.reshape(total_tok, HEADS, HD).astype(jnp.float32)
    fast_keys = (attended * lax.rsqrt(lax.optimization_barrier(jnp.mean(attended * attended, -1, keepdims=True)) + 1e-06)).astype(jnp.bfloat16)
    tok_index = jnp.arange(NR * COLS, dtype=jnp.int32)
    valid_mask = (tok_index[None, :] < view_counts[:, None]).reshape(total_tok).astype(jnp.float32)
    rates_tok = jnp.transpose(token_rates, (0, 2, 1)).reshape(total_tok, HEADS)
    scaled = (rates_tok[:, :, None] * valid_mask[:, None, None] * target.reshape(total_tok, HEADS, HD).astype(jnp.float32)).astype(jnp.bfloat16)
    total_valid = jnp.sum(view_counts).astype(jnp.float32)
    results = []
    for head in range(HEADS):
        key_rows = fast_keys[:, head]
        scaled_rows = scaled[:, head]
        first_proj = jnp.dot(key_rows, w_first[head], preferred_element_type=jnp.float32)
        third_proj = jnp.dot(key_rows, w_third[head], preferred_element_type=jnp.float32)
        gated_rows = (jax.nn.silu(first_proj) * third_proj).astype(jnp.bfloat16)
        back_rows = lax.dot_general(scaled_rows, w_second[head], (((1,), (1,)), ((), ())), preferred_element_type=jnp.float32)
        back_first = (back_rows * third_proj * silu_slope(first_proj)).astype(jnp.bfloat16)
        back_third = (back_rows * jax.nn.silu(first_proj)).astype(jnp.bfloat16)
        grad_first = jnp.dot(key_rows.T, back_first, preferred_element_type=jnp.float32)
        grad_third = jnp.dot(key_rows.T, back_third, preferred_element_type=jnp.float32)
        grad_second = jnp.dot(gated_rows.T, scaled_rows, preferred_element_type=jnp.float32)
        new_first = renorm(w_first[head], grad_first, total_valid)
        new_third = renorm(w_third[head], grad_third, total_valid)
        new_second = renorm(w_second[head], grad_second, total_valid)
        applied = (jax.nn.silu(jnp.dot(key_rows, new_first, preferred_element_type=jnp.float32)) * jnp.dot(key_rows, new_third, preferred_element_type=jnp.float32)).astype(jnp.bfloat16)
        results.append(jnp.dot(applied, new_second, preferred_element_type=jnp.float32).astype(jnp.bfloat16))
    return jnp.stack(results, 1).reshape(VIEWS, NR, COLS, HEADS * HD)
```

```python
import functools
import math

import jax
import jax.numpy as jnp
from jax import lax
from jax.experimental import pallas as pl
from jax.experimental.pallas import tpu as pltpu
from jax.sharding import PartitionSpec as P

HD = 512
ATT_HD = 128
HALO = 2
MESH = pl.DeviceIdType.MESH
BF16 = jnp.bfloat16
F32 = jnp.float32
NT = (((1,), (1,)), ((), ()))
TN = (((0,), (0,)), ((), ()))


def with_halo(value, sides, width):
    for axis, dim in sides:
        size, length = (lax.axis_size(axis), value.shape[dim])
        up = [(i, (i + 1) % size) for i in range(size - 1)]
        down = [(j, i) for i, j in up]
        last = lax.slice_in_dim(value, length - width, length, axis=dim)
        leading = lax.slice_in_dim(value, 0, width, axis=dim)
        before = lax.ppermute(last, axis, up)
        after = lax.ppermute(leading, axis, down)
        value = jnp.concatenate([before, value, after], axis=dim)
    return value


def silu_slope(values_in):
    sigmoid_x = jax.nn.sigmoid(values_in)
    return sigmoid_x * (1.0 + values_in * (1.0 - sigmoid_x))


def attend(
    query_rows,
    key_rows,
    value_rows,
    q_row_ids,
    k_row_ids,
    q_tok,
    k_tok,
    k_valid,
    q_reach,
    grid_rows,
):
    count_q = query_rows.shape[0]
    count_k = key_rows.shape[0]
    groups = query_rows.shape[1] // ATT_HD
    query_heads = query_rows.reshape(count_q, groups, ATT_HD)
    key_heads = key_rows.reshape(count_k, groups, ATT_HD)
    value_heads = value_rows.reshape(count_k, groups, ATT_HD)
    scores = jnp.einsum(
        "qhd,khd->hqk", query_heads, key_heads, preferred_element_type=jnp.float32
    ) / math.sqrt(ATT_HD)
    inside = (k_row_ids >= 0) & (k_row_ids < grid_rows)
    in_band = jnp.abs(k_row_ids[None, :] - q_row_ids[:, None]) <= q_reach[:, None]
    allowed = in_band & inside[None, :] & (k_valid[None, :] | (k_tok[None, :] == q_tok[:, None]))
    scores = jnp.where(allowed[None], scores, -1e30)
    row_top = jnp.max(scores, -1, keepdims=True)
    powers = jnp.exp(scores - row_top)
    weights = (powers / jnp.sum(powers, -1, keepdims=True)).astype(jnp.bfloat16)
    output_rows = jnp.einsum(
        "hqk,khd->qhd", weights, value_heads, preferred_element_type=jnp.float32
    )
    return output_rows.reshape(count_q, groups * ATT_HD).astype(jnp.bfloat16)


def renorm(old_matrix, grad, total_valid):
    old_rows = old_matrix.astype(jnp.float32)
    raised = old_rows + grad / total_valid
    rescale = jnp.sqrt(jnp.sum(old_rows * old_rows, -1, keepdims=True) + 1e-06) / jnp.sqrt(
        jnp.sum(raised * raised, -1, keepdims=True) + 1e-06
    )
    return (raised * rescale).astype(jnp.bfloat16)


def per_device(
    query_feats,
    key_feats,
    value_feats,
    target,
    token_rates,
    row_reach,
    view_counts,
    w_first,
    w_third,
    w_second,
):
    row_count = query_feats.shape[1]
    col_count = query_feats.shape[2]
    feat_width = query_feats.shape[3]
    heads_here = feat_width // HD
    tokens_here = row_count * col_count
    key_span = row_count + 2 * HALO
    grid_rows = lax.axis_size("row") * row_count
    row_base = lax.axis_index("row") * row_count
    view_total = view_counts[0]
    total_valid = lax.psum(view_total.astype(jnp.float32), "view")
    paired = jnp.stack([key_feats[0], value_feats[0]], 0)
    padded = with_halo(paired, (("row", 1),), HALO)
    q_row_ids = row_base + jnp.repeat(jnp.arange(row_count, dtype=jnp.int32), col_count)
    k_row_ids = row_base - HALO + jnp.repeat(jnp.arange(key_span, dtype=jnp.int32), col_count)
    q_tok = q_row_ids * col_count + jnp.tile(jnp.arange(col_count, dtype=jnp.int32), row_count)
    k_tok = k_row_ids * col_count + jnp.tile(jnp.arange(col_count, dtype=jnp.int32), key_span)
    k_valid = k_tok < view_total
    q_reach = jnp.repeat(row_reach, col_count)
    attended = attend(
        query_feats[0].reshape(tokens_here, feat_width),
        padded[0].reshape(key_span * col_count, feat_width),
        padded[1].reshape(key_span * col_count, feat_width),
        q_row_ids,
        k_row_ids,
        q_tok,
        k_tok,
        k_valid,
        q_reach,
        grid_rows,
    )
    attended = attended.reshape(tokens_here, heads_here, HD).astype(jnp.float32)
    fast_keys = (
        attended * lax.rsqrt(jnp.mean(attended * attended, -1, keepdims=True) + 1e-06)
    ).astype(jnp.bfloat16)
    valid_mask = (q_tok < view_total).astype(jnp.float32)
    rates_tok = token_rates[0].T
    scaled = (
        rates_tok[:, :, None]
        * valid_mask[:, None, None]
        * target[0].reshape(tokens_here, heads_here, HD).astype(jnp.float32)
    ).astype(jnp.bfloat16)
    first_proj = jnp.einsum("thi,hij->thj", fast_keys, w_first, preferred_element_type=jnp.float32)
    third_proj = jnp.einsum("thi,hij->thj", fast_keys, w_third, preferred_element_type=jnp.float32)
    gated_rows = (jax.nn.silu(first_proj) * third_proj).astype(jnp.bfloat16)
    back_rows = jnp.einsum("tho,hjo->thj", scaled, w_second, preferred_element_type=jnp.float32)
    back_first = (back_rows * third_proj * silu_slope(first_proj)).astype(jnp.bfloat16)
    back_third = (back_rows * jax.nn.silu(first_proj)).astype(jnp.bfloat16)
    grad_first = jnp.einsum(
        "thi,thj->hij", fast_keys, back_first, preferred_element_type=jnp.float32
    )
    grad_third = jnp.einsum(
        "thi,thj->hij", fast_keys, back_third, preferred_element_type=jnp.float32
    )
    grad_second = jnp.einsum("thj,tho->hjo", gated_rows, scaled, preferred_element_type=jnp.float32)
    grad_first, grad_third, grad_second = lax.psum(
        (grad_first, grad_third, grad_second), ("view", "row")
    )
    new_first = renorm(w_first, grad_first, total_valid)
    new_third = renorm(w_third, grad_third, total_valid)
    new_second = renorm(w_second, grad_second, total_valid)
    applied = (
        jax.nn.silu(
            jnp.einsum("thi,hij->thj", fast_keys, new_first, preferred_element_type=jnp.float32)
        )
        * jnp.einsum("thi,hij->thj", fast_keys, new_third, preferred_element_type=jnp.float32)
    ).astype(jnp.bfloat16)
    fast_out = jnp.einsum(
        "thj,hjo->tho", applied, new_second, preferred_element_type=jnp.float32
    ).astype(jnp.bfloat16)
    return fast_out.reshape(1, row_count, col_count, feat_width)


def halve(values_in, size):
    if size & (size - 1) == 0:
        return values_in >> (size.bit_length() - 1)
    return lax.div(values_in, jnp.int32(size))


def dot(left, right, dims=(((1,), (0,)), ((), ()))):
    return lax.dot_general(left, right, dims, preferred_element_type=F32)


def lane_square_sums(matrix):
    wide = matrix.astype(F32)
    square = wide * wide
    high = square.astype(BF16)
    low = (square - high.astype(F32)).astype(BF16)
    ones = jnp.ones((8, matrix.shape[1]), BF16)
    return dot(ones, high, NT) + dot(ones, low, NT)


def step_kernel(
    nr, nz, cols,
    q_ref, k_ref, v_ref, t_ref, rates_ref, reach_ref, count_ref, wf_hbm, wt_hbm, ws_hbm,
    out_ref,
    wf, wt, ws, halo, kall, sall, fac, fac_send, cnt, gfull, gsend, grecv,
    wtr, news, ss, ssz, osend, orecv, load_sem, send_sem, recv_sem,
):
    tokens, width = q_ref.shape
    rows_here = tokens // cols
    hid = width // nr
    part = hid // nz
    edge = HALO * cols
    me = lax.axis_index("row")
    mz = lax.axis_index("view")

    loads = [
        pltpu.make_async_copy(source, target, load_sem.at[i])
        for i, (source, target) in enumerate(((wf_hbm, wf), (wt_hbm, wt), (ws_hbm, ws)))
    ]
    for load in loads:
        load.start()

    def row_peer(shift):
        return lax.rem(me + (shift + nr), nr)

    def view_peer(shift):
        return lax.rem(mz + (shift + nz), nz)

    used = [0]

    def send(source, target, axis, peer):
        slot = used[0]
        used[0] += 1
        copy = pltpu.make_async_remote_copy(
            src_ref=source, dst_ref=target,
            send_sem=send_sem.at[slot], recv_sem=recv_sem.at[slot],
            device_id={axis: peer}, device_id_type=MESH,
        )
        copy.start()
        return copy

    barrier = pltpu.get_barrier_semaphore()
    for d in range(1, nr):
        pl.semaphore_signal(barrier, inc=1, device_id={"row": row_peer(d)}, device_id_type=MESH)
    for d in range(1, nz):
        pl.semaphore_signal(barrier, inc=1, device_id={"view": view_peer(d)}, device_id_type=MESH)

    row_base = me * rows_here
    tok_base = me * tokens
    view_total = count_ref[0]
    sub = lax.broadcasted_iota(jnp.int32, (tokens, tokens), 0)
    lane = lax.broadcasted_iota(jnp.int32, (tokens, tokens), 1)
    rate_col = jnp.sum(jnp.where(sub == lane, rates_ref[...], 0.0), axis=1, keepdims=True)
    tok_col = tok_base + lax.broadcasted_iota(jnp.int32, (tokens, 1), 0)
    valid_col = (tok_col < view_total).astype(F32)
    sall[0] = (rate_col * valid_col * t_ref[...].astype(F32)).astype(BF16)
    cnt[0] = jnp.full((8, 128), view_total, jnp.int32).astype(F32)

    pl.semaphore_wait(barrier, (nr - 1) + (nz - 1))

    halo_copies = []
    for i, ref in enumerate((k_ref, v_ref)):
        halo_copies.append(send(ref.at[pl.ds(tokens - edge, edge)], halo.at[0, i], "row", row_peer(1)))
        halo_copies.append(send(ref.at[pl.ds(0, edge)], halo.at[1, i], "row", row_peer(-1)))
    s_copies = [send(sall.at[0], sall.at[d], "row", row_peer(d)) for d in range(1, nr)]
    c_copies = [send(cnt.at[0], cnt.at[d], "view", view_peer(d)) for d in range(1, nz)]

    span = tokens + 2 * edge
    qi = lax.broadcasted_iota(jnp.int32, (tokens, span), 0)
    ki = lax.broadcasted_iota(jnp.int32, (tokens, span), 1)
    q_row = halve(qi, cols)
    k_row = halve(ki, cols) - HALO
    reach = jnp.zeros((tokens, span), jnp.int32)
    for r in range(rows_here):
        reach = jnp.where(q_row == r, reach_ref[r], reach)
    k_abs = k_row + row_base
    k_tok = ki - edge
    allowed = (
        (jnp.abs(k_row - q_row) <= reach)
        & (k_abs >= 0)
        & (k_abs < nr * rows_here)
        & ((k_tok + tok_base < view_total) | (k_tok == qi))
    )
    for copy in halo_copies:
        copy.wait()
    pieces = []
    total_sq = jnp.zeros((tokens, 1), F32)
    for h in range(width // ATT_HD):
        hs = slice(h * ATT_HD, (h + 1) * ATT_HD)
        keys = jnp.concatenate([halo[0, 0, :, hs], k_ref[:, hs], halo[1, 0, :, hs]], axis=0)
        vals = jnp.concatenate([halo[0, 1, :, hs], v_ref[:, hs], halo[1, 1, :, hs]], axis=0)
        scores = dot(q_ref[:, hs], keys, NT) * (1.0 / math.sqrt(ATT_HD))
        scores = jnp.where(allowed, scores, -1e30)
        powers = jnp.exp(scores - jnp.max(scores, axis=-1, keepdims=True))
        weights = (powers * (1.0 / jnp.sum(powers, axis=-1, keepdims=True))).astype(BF16)
        piece = dot(weights, vals).astype(BF16).astype(F32)
        total_sq = total_sq + jnp.sum(piece * piece, axis=-1, keepdims=True)
        pieces.append(piece)
    norm = lax.rsqrt(total_sq * (1.0 / width) + 1e-06)
    for h, piece in enumerate(pieces):
        kall[0, :, h * ATT_HD:(h + 1) * ATT_HD] = (piece * norm).astype(BF16)
    k_copies = [send(kall.at[0], kall.at[d], "row", row_peer(d)) for d in range(1, nr)]

    for load in loads:
        load.wait()
    f_copies = []
    for d in list(range(1, nr)) + [0]:
        mine = pl.ds(pl.multiple_of(row_peer(d) * hid, hid), hid)
        first = dot(kall[0], wf[:, mine])
        third = dot(kall[0], wt[:, mine])
        back = dot(sall[0], ws[mine, :], NT)
        sig = jax.nn.sigmoid(first)
        gate = first * sig
        parts = (
            (back * third * (sig * (1.0 + first * (1.0 - sig)))).astype(BF16),
            (back * gate).astype(BF16),
            (gate * third).astype(BF16),
        )
        for m in range(3):
            if d:
                fac_send[d - 1, m] = parts[m]
            else:
                fac[0, m] = parts[m]
        if d:
            f_copies.append(send(fac_send.at[d - 1], fac.at[d], "row", row_peer(d)))

    mine = pl.ds(pl.multiple_of(me * hid, hid), hid)
    wtr[0] = wf[:, mine].astype(F32).T
    wtr[1] = wt[:, mine].astype(F32).T
    wtr[2] = ws[mine, :].astype(F32)
    old_sums = [lane_square_sums(wf[...]), lane_square_sums(wt[...])]

    for copy in s_copies + k_copies + f_copies:
        copy.wait()

    g_copies = []
    for m in (2, 0, 1):
        right = sall if m == 2 else kall
        grad = dot(fac[0, m], right[0], TN)
        for d in range(1, nr):
            grad = grad + dot(fac[d, m], right[d], TN)
        gfull[m] = grad
        for z in range(nz):
            gsend[z, m] = grad[z * part:(z + 1) * part].astype(BF16)
        for d in range(1, nz):
            g_copies.append(
                send(gsend.at[view_peer(d), m], grecv.at[d - 1, m], "view", view_peer(d))
            )
    for copy in c_copies:
        copy.wait()
    total_valid = cnt[0, 0:1, 0:1]
    for d in range(1, nz):
        total_valid = total_valid + cnt[d, 0:1, 0:1]

    here = pl.ds(pl.multiple_of(mz * part, part), part)
    w_copies = []
    sums = []
    for i, m in enumerate((2, 0, 1)):
        for copy in g_copies[i * (nz - 1):(i + 1) * (nz - 1)]:
            copy.wait()
        grad = gfull[m, here, :]
        for d in range(1, nz):
            grad = grad + grecv[d - 1, m].astype(F32)
        old = wtr[m, here, :]
        raised = old + grad / total_valid
        if m == 2:
            rescale = jnp.sqrt(jnp.sum(old * old, -1, keepdims=True) + 1e-06) / jnp.sqrt(
                jnp.sum(raised * raised, -1, keepdims=True) + 1e-06
            )
            raised = raised * rescale
        else:
            sums.append(jnp.sum(raised * raised, axis=0, keepdims=True))
        news[0, m] = raised.astype(BF16)
        for d in range(1, nz):
            w_copies.append(send(news.at[0, m], news.at[d, m], "view", view_peer(d)))
    ss[0, 0:1] = sums[0]
    ss[0, 1:2] = sums[1]
    ss_copies = [send(ss.at[0], ss.at[d], "row", row_peer(d)) for d in range(1, nr)]
    for copy in ss_copies:
        copy.wait()
    strip_sums = ss[0, 0:2]
    for d in range(1, nr):
        strip_sums = strip_sums + ss[d, 0:2]
    ssz[0, 0:2] = strip_sums
    ssz_copies = [send(ssz.at[0], ssz.at[d], "view", view_peer(d)) for d in range(1, nz)]
    for copy in ssz_copies:
        copy.wait()
    new_sums = ssz[0, 0:2]
    for d in range(1, nz):
        new_sums = new_sums + ssz[d, 0:2]
    scale_first = jnp.sqrt(old_sums[0][0:1] + 1e-06) / jnp.sqrt(new_sums[0:1] + 1e-06)
    scale_third = jnp.sqrt(old_sums[1][0:1] + 1e-06) / jnp.sqrt(new_sums[1:2] + 1e-06)

    for copy in w_copies:
        copy.wait()
    new_first, new_third, new_second = (
        jnp.concatenate([news[d, m] for d in range(nz)], axis=0) for m in range(3)
    )
    o_copies = []
    for d in list(range(1, nr)) + [0]:
        keys = kall[d].astype(F32)
        first = dot((keys * scale_first).astype(BF16), new_first, NT)
        third = dot((keys * scale_third).astype(BF16), new_third, NT)
        applied = (first * jax.nn.sigmoid(first) * third).astype(BF16)
        share = dot(applied, new_second)
        if d:
            osend[d - 1] = share.astype(BF16)
            o_copies.append(send(osend.at[d - 1], orecv.at[d - 1], "row", row_peer(-d)))
    for copy in o_copies:
        copy.wait()
    for d in range(1, nr):
        share = share + orecv[d - 1].astype(F32)
    out_ref[...] = share.astype(BF16)


def fused_step(
    nr, nz,
    query_feats, key_feats, value_feats, target, token_rates, row_reach, view_counts,
    w_first, w_third, w_second,
):
    _, row_count, cols, width = query_feats.shape
    tokens = row_count * cols
    hid = width // nr
    part = hid // nz
    edge = HALO * cols
    copies = 4 + 3 * (nr - 1) + (nz - 1) + 3 * (nz - 1) + 3 * (nz - 1) + (nr - 1) + (nz - 1) + (nr - 1)
    vmem = pl.BlockSpec(memory_space=pltpu.VMEM)
    smem = pl.BlockSpec(memory_space=pltpu.SMEM)
    anywhere = pl.BlockSpec(memory_space=pl.ANY)
    flat = lambda a: a.reshape(tokens, width)
    out = pl.pallas_call(
        functools.partial(step_kernel, nr, nz, cols),
        out_shape=jax.ShapeDtypeStruct((tokens, width), BF16),
        in_specs=[vmem] * 5 + [smem] * 2 + [anywhere] * 3,
        out_specs=vmem,
        scratch_shapes=[
            pltpu.VMEM((width, width), BF16),
            pltpu.VMEM((width, width), BF16),
            pltpu.VMEM((width, width), BF16),
            pltpu.VMEM((2, 2, edge, width), BF16),
            pltpu.VMEM((nr, tokens, width), BF16),
            pltpu.VMEM((nr, tokens, width), BF16),
            pltpu.VMEM((nr, 3, tokens, hid), BF16),
            pltpu.VMEM((nr - 1, 3, tokens, hid), BF16),
            pltpu.VMEM((nz, 8, 128), F32),
            pltpu.VMEM((3, hid, width), F32),
            pltpu.VMEM((nz, 3, part, width), BF16),
            pltpu.VMEM((nz - 1, 3, part, width), BF16),
            pltpu.VMEM((3, hid, width), F32),
            pltpu.VMEM((nz, 3, part, width), BF16),
            pltpu.VMEM((nr, 8, width), F32),
            pltpu.VMEM((nz, 8, width), F32),
            pltpu.VMEM((nr - 1, tokens, width), BF16),
            pltpu.VMEM((nr - 1, tokens, width), BF16),
            pltpu.SemaphoreType.DMA((3,)),
            pltpu.SemaphoreType.DMA((copies,)),
            pltpu.SemaphoreType.DMA((copies,)),
        ],
        compiler_params=pltpu.CompilerParams(collective_id=0, has_side_effects=True),
    )(
        flat(query_feats), flat(key_feats), flat(value_feats), flat(target),
        token_rates.reshape(1, tokens), row_reach, view_counts,
        w_first.reshape(width, width), w_third.reshape(width, width), w_second.reshape(width, width),
    )
    return out.reshape(query_feats.shape)


def solution(mesh):
    placed = (
        P("view", "row", None, "head"),
        P("view", "row", None, "head"),
        P("view", "row", None, "head"),
        P("view", "row", None, "head"),
        P("view", "head", "row"),
        P("row"),
        P("view"),
        P("head", None, None),
        P("head", None, None),
        P("head", None, None),
    )
    nr, nz = mesh.shape["row"], mesh.shape["view"]
    fits = nr > 1 and nz > 1 and HD % (128 * nr) == 0 and HD % (16 * nr * nz) == 0
    return jax.shard_map(
        functools.partial(fused_step, nr, nz) if fits else per_device,
        mesh=mesh,
        in_specs=placed,
        out_specs=P("view", "row", None, "head"),
        check_vma=False,
    )
```

```python
import functools
import math

import jax
import jax.numpy as jnp
from jax import lax
from jax.experimental import pallas as pl
from jax.experimental.pallas import tpu as pltpu
from jax.sharding import PartitionSpec as P

HD = 512
ATT_HD = 128
HALO = 2
MESH = pl.DeviceIdType.MESH
BF16 = jnp.bfloat16
F32 = jnp.float32
NT = (((1,), (1,)), ((), ()))
TN = (((0,), (0,)), ((), ()))


def with_halo(value, sides, width):
    for axis, dim in sides:
        size, length = (lax.axis_size(axis), value.shape[dim])
        up = [(i, (i + 1) % size) for i in range(size - 1)]
        down = [(j, i) for i, j in up]
        last = lax.slice_in_dim(value, length - width, length, axis=dim)
        leading = lax.slice_in_dim(value, 0, width, axis=dim)
        before = lax.ppermute(last, axis, up)
        after = lax.ppermute(leading, axis, down)
        value = jnp.concatenate([before, value, after], axis=dim)
    return value


def silu_slope(values_in):
    sigmoid_x = jax.nn.sigmoid(values_in)
    return sigmoid_x * (1.0 + values_in * (1.0 - sigmoid_x))


def attend(
    query_rows,
    key_rows,
    value_rows,
    q_row_ids,
    k_row_ids,
    q_tok,
    k_tok,
    k_valid,
    q_reach,
    grid_rows,
):
    count_q = query_rows.shape[0]
    count_k = key_rows.shape[0]
    groups = query_rows.shape[1] // ATT_HD
    query_heads = query_rows.reshape(count_q, groups, ATT_HD)
    key_heads = key_rows.reshape(count_k, groups, ATT_HD)
    value_heads = value_rows.reshape(count_k, groups, ATT_HD)
    scores = jnp.einsum(
        "qhd,khd->hqk", query_heads, key_heads, preferred_element_type=jnp.float32
    ) / math.sqrt(ATT_HD)
    inside = (k_row_ids >= 0) & (k_row_ids < grid_rows)
    in_band = jnp.abs(k_row_ids[None, :] - q_row_ids[:, None]) <= q_reach[:, None]
    allowed = in_band & inside[None, :] & (k_valid[None, :] | (k_tok[None, :] == q_tok[:, None]))
    scores = jnp.where(allowed[None], scores, -1e30)
    row_top = jnp.max(scores, -1, keepdims=True)
    powers = jnp.exp(scores - row_top)
    weights = (powers / jnp.sum(powers, -1, keepdims=True)).astype(jnp.bfloat16)
    output_rows = jnp.einsum(
        "hqk,khd->qhd", weights, value_heads, preferred_element_type=jnp.float32
    )
    return output_rows.reshape(count_q, groups * ATT_HD).astype(jnp.bfloat16)


def renorm(old_matrix, grad, total_valid):
    old_rows = old_matrix.astype(jnp.float32)
    raised = old_rows + grad / total_valid
    rescale = jnp.sqrt(jnp.sum(old_rows * old_rows, -1, keepdims=True) + 1e-06) / jnp.sqrt(
        jnp.sum(raised * raised, -1, keepdims=True) + 1e-06
    )
    return (raised * rescale).astype(jnp.bfloat16)


def per_device(
    query_feats,
    key_feats,
    value_feats,
    target,
    token_rates,
    row_reach,
    view_counts,
    w_first,
    w_third,
    w_second,
):
    row_count = query_feats.shape[1]
    col_count = query_feats.shape[2]
    feat_width = query_feats.shape[3]
    heads_here = feat_width // HD
    tokens_here = row_count * col_count
    key_span = row_count + 2 * HALO
    grid_rows = lax.axis_size("row") * row_count
    row_base = lax.axis_index("row") * row_count
    view_total = view_counts[0]
    total_valid = lax.psum(view_total.astype(jnp.float32), "view")
    paired = jnp.stack([key_feats[0], value_feats[0]], 0)
    padded = with_halo(paired, (("row", 1),), HALO)
    q_row_ids = row_base + jnp.repeat(jnp.arange(row_count, dtype=jnp.int32), col_count)
    k_row_ids = row_base - HALO + jnp.repeat(jnp.arange(key_span, dtype=jnp.int32), col_count)
    q_tok = q_row_ids * col_count + jnp.tile(jnp.arange(col_count, dtype=jnp.int32), row_count)
    k_tok = k_row_ids * col_count + jnp.tile(jnp.arange(col_count, dtype=jnp.int32), key_span)
    k_valid = k_tok < view_total
    q_reach = jnp.repeat(row_reach, col_count)
    attended = attend(
        query_feats[0].reshape(tokens_here, feat_width),
        padded[0].reshape(key_span * col_count, feat_width),
        padded[1].reshape(key_span * col_count, feat_width),
        q_row_ids,
        k_row_ids,
        q_tok,
        k_tok,
        k_valid,
        q_reach,
        grid_rows,
    )
    attended = attended.reshape(tokens_here, heads_here, HD).astype(jnp.float32)
    fast_keys = (
        attended * lax.rsqrt(jnp.mean(attended * attended, -1, keepdims=True) + 1e-06)
    ).astype(jnp.bfloat16)
    valid_mask = (q_tok < view_total).astype(jnp.float32)
    rates_tok = token_rates[0].T
    scaled = (
        rates_tok[:, :, None]
        * valid_mask[:, None, None]
        * target[0].reshape(tokens_here, heads_here, HD).astype(jnp.float32)
    ).astype(jnp.bfloat16)
    first_proj = jnp.einsum("thi,hij->thj", fast_keys, w_first, preferred_element_type=jnp.float32)
    third_proj = jnp.einsum("thi,hij->thj", fast_keys, w_third, preferred_element_type=jnp.float32)
    gated_rows = (jax.nn.silu(first_proj) * third_proj).astype(jnp.bfloat16)
    back_rows = jnp.einsum("tho,hjo->thj", scaled, w_second, preferred_element_type=jnp.float32)
    back_first = (back_rows * third_proj * silu_slope(first_proj)).astype(jnp.bfloat16)
    back_third = (back_rows * jax.nn.silu(first_proj)).astype(jnp.bfloat16)
    grad_first = jnp.einsum(
        "thi,thj->hij", fast_keys, back_first, preferred_element_type=jnp.float32
    )
    grad_third = jnp.einsum(
        "thi,thj->hij", fast_keys, back_third, preferred_element_type=jnp.float32
    )
    grad_second = jnp.einsum("thj,tho->hjo", gated_rows, scaled, preferred_element_type=jnp.float32)
    grad_first, grad_third, grad_second = lax.psum(
        (grad_first, grad_third, grad_second), ("view", "row")
    )
    new_first = renorm(w_first, grad_first, total_valid)
    new_third = renorm(w_third, grad_third, total_valid)
    new_second = renorm(w_second, grad_second, total_valid)
    applied = (
        jax.nn.silu(
            jnp.einsum("thi,hij->thj", fast_keys, new_first, preferred_element_type=jnp.float32)
        )
        * jnp.einsum("thi,hij->thj", fast_keys, new_third, preferred_element_type=jnp.float32)
    ).astype(jnp.bfloat16)
    fast_out = jnp.einsum(
        "thj,hjo->tho", applied, new_second, preferred_element_type=jnp.float32
    ).astype(jnp.bfloat16)
    return fast_out.reshape(1, row_count, col_count, feat_width)


def halve(values_in, size):
    if size & (size - 1) == 0:
        return values_in >> (size.bit_length() - 1)
    return lax.div(values_in, jnp.int32(size))


def dot(left, right, dims=(((1,), (0,)), ((), ()))):
    return lax.dot_general(left, right, dims, preferred_element_type=F32)


def flip(index, bits):
    bit = 1
    while bit <= bits:
        if bits & bit:
            index = index + bit - 2 * bit * lax.rem(lax.div(index, bit), 2)
        bit *= 2
    return index


def step_kernel(
    nr, nz, cols,
    q_hbm, k_hbm, v_hbm, t_hbm, rates_hbm, reach_ref, count_ref, wf_hbm, wt_hbm, ws_hbm,
    out_ref,
    q_ref, k_ref, v_ref, t_ref, rates_ref, wf, wt, ws, halo, kall, sall, cnt, gfull, gsend, grecv,
    wtr, news, ss, ssz, osend, orecv, load_sem, send_sem, recv_sem,
):
    tokens, width = q_ref.shape
    rows_here = tokens // cols
    hid = width // nr
    part = hid // nz
    edge = HALO * cols
    heads = width // ATT_HD
    me = lax.axis_index("row")
    mz = lax.axis_index("view")
    mine = pl.ds(pl.multiple_of(me * hid, hid), hid)
    here = pl.ds(pl.multiple_of(mz * part, part), part)

    loads = [
        pltpu.make_async_copy(source, target, load_sem.at[i])
        for i, (source, target) in enumerate((
            (k_hbm, k_ref), (v_hbm, v_ref), (t_hbm, t_ref), (rates_hbm, rates_ref), (q_hbm, q_ref),
            (wf_hbm.at[:, mine], wf), (wt_hbm.at[:, mine], wt), (ws_hbm.at[mine, :], ws),
        ))
    ]
    for load in loads:
        load.start()

    def view_peer(shift):
        return lax.rem(mz + (shift + nz), nz)

    used = [0]

    def send(source, target, axis, peer):
        slot = used[0]
        used[0] += 1
        copy = pltpu.make_async_remote_copy(
            src_ref=source, dst_ref=target,
            send_sem=send_sem.at[slot], recv_sem=recv_sem.at[slot],
            device_id={axis: peer}, device_id_type=MESH,
        )
        copy.start()
        return copy

    def spread(ref):
        return {d: send(ref.at[0], ref.at[d], "row", flip(me, d)) for d in [1] + list(range(2, nr, 2))}

    def hand_on(ref, copies):
        for d in range(2, nr, 2):
            copies[d].wait_recv()
            copies[d + 1] = send(ref.at[d], ref.at[d + 1], "row", flip(me, 1))

    def settle(copies):
        for d in copies:
            copies[d].wait_send()

    barrier = pltpu.get_barrier_semaphore()
    for d in range(1, nr):
        pl.semaphore_signal(barrier, inc=1, device_id={"row": flip(me, d)}, device_id_type=MESH)
    for d in range(1, nz):
        pl.semaphore_signal(barrier, inc=1, device_id={"view": view_peer(d)}, device_id_type=MESH)
    above = lax.rem(me + 1, nr)
    below = lax.rem(me + (nr - 1), nr)

    row_base = me * rows_here
    tok_base = me * tokens
    view_total = count_ref[0]
    cnt[0] = jnp.full((8, 128), view_total, jnp.int32).astype(F32)
    sub = lax.broadcasted_iota(jnp.int32, (tokens, tokens), 0)
    lane = lax.broadcasted_iota(jnp.int32, (tokens, tokens), 1)
    tok_col = tok_base + lax.broadcasted_iota(jnp.int32, (tokens, 1), 0)
    valid_col = (tok_col < view_total).astype(F32)
    for load in loads[2:4]:
        load.wait()
    rate_col = jnp.sum(jnp.where(sub == lane, rates_ref[...], 0.0), axis=1, keepdims=True)
    sall[0] = (rate_col * valid_col * t_ref[...].astype(F32)).astype(BF16)
    for load in loads[:2]:
        load.wait()

    pl.semaphore_wait(barrier, (nr - 1) + (nz - 1))

    halo_copies = []
    for i, ref in enumerate((k_ref, v_ref)):
        halo_copies.append(send(ref.at[pl.ds(tokens - edge, edge)], halo.at[i, pl.ds(0, edge)], "row", above))
        halo_copies.append(send(ref.at[pl.ds(0, edge)], halo.at[i, pl.ds(edge, edge)], "row", below))
    s_copies = spread(sall)
    c_copies = [send(cnt.at[0], cnt.at[d], "view", view_peer(d)) for d in range(1, nz)]

    def allowed(q_tok, k_tok):
        q_row = halve(q_tok, cols)
        k_row = halve(k_tok + edge, cols) - HALO
        reach = jnp.zeros(q_tok.shape, jnp.int32)
        for r in range(rows_here):
            reach = jnp.where(q_row == r, reach_ref[r], reach)
        k_abs = k_row + row_base
        return (
            (jnp.abs(k_row - q_row) <= reach)
            & (k_abs >= 0)
            & (k_abs < nr * rows_here)
            & ((k_tok + tok_base < view_total) | (k_tok == q_tok))
        )

    near_ok = allowed(sub, lane)
    far_q = lax.broadcasted_iota(jnp.int32, (tokens, 2 * edge), 0)
    far_k = lax.broadcasted_iota(jnp.int32, (tokens, 2 * edge), 1)
    far_ok = allowed(far_q, jnp.where(far_k < edge, far_k - edge, far_k - edge + tokens))
    root = 1.0 / math.sqrt(ATT_HD)
    spans = [slice(h * ATT_HD, (h + 1) * ATT_HD) for h in range(heads)]
    loads[4].wait()
    near = [
        jnp.where(near_ok, dot(q_ref[:, hs], k_ref[:, hs], NT) * root, -1e30) for hs in spans
    ]
    near_top = [jnp.max(scores, axis=-1, keepdims=True) for scores in near]
    for load in loads[5:]:
        load.wait()
    wtr[0] = wf[...].astype(F32).T
    wtr[1] = wt[...].astype(F32).T
    wtr[2] = ws[...].astype(F32)
    for copy in halo_copies:
        copy.wait()
    pieces = []
    total_sq = jnp.zeros((tokens, 1), F32)
    for h, hs in enumerate(spans):
        far = jnp.where(far_ok, dot(q_ref[:, hs], halo[0, :, hs], NT) * root, -1e30)
        top = jnp.maximum(near_top[h], jnp.max(far, axis=-1, keepdims=True))
        near_pow = jnp.exp(near[h] - top)
        far_pow = jnp.exp(far - top)
        inverse = 1.0 / (
            jnp.sum(near_pow, axis=-1, keepdims=True) + jnp.sum(far_pow, axis=-1, keepdims=True)
        )
        piece = dot((near_pow * inverse).astype(BF16), v_ref[:, hs]) + dot(
            (far_pow * inverse).astype(BF16), halo[1, :, hs]
        )
        piece = piece.astype(BF16).astype(F32)
        total_sq = total_sq + jnp.sum(piece * piece, axis=-1, keepdims=True)
        pieces.append(piece)
    norm = lax.rsqrt(total_sq * (1.0 / width) + 1e-06)
    for hs, piece in zip(spans, pieces):
        kall[0, :, hs] = (piece * norm).astype(BF16)
    k_copies = spread(kall)
    hand_on(sall, s_copies)

    def gradients(d):
        first = dot(kall[d], wf[...])
        third = dot(kall[d], wt[...])
        back = dot(sall[d], ws[...], NT)
        sig = jax.nn.sigmoid(first)
        gate = first * sig
        return (
            dot((back * third * (sig * (1.0 + first * (1.0 - sig)))).astype(BF16), kall[d], TN),
            dot((back * gate).astype(BF16), kall[d], TN),
            dot((gate * third).astype(BF16), sall[d], TN),
        )

    for m, grad in enumerate(gradients(0)):
        gfull[m] = grad
    for d in [1] + list(range(2, nr, 2)) + list(range(3, nr, 2)):
        if d == 2:
            hand_on(kall, k_copies)
        if d % 2:
            k_copies[d].wait_recv()
            s_copies[d].wait_recv()
        for m, grad in enumerate(gradients(d)):
            gfull[m] += grad
    g_copies = []
    for m in range(3):
        for z in range(nz):
            gsend[z, m] = gfull[m, z * part:(z + 1) * part, :].astype(BF16)
        for d in range(1, nz):
            g_copies.append(
                send(gsend.at[view_peer(d), m], grecv.at[d - 1, m], "view", view_peer(d))
            )
    ss[0, 2:3] = jnp.sum(wtr[0] * wtr[0], axis=0, keepdims=True)
    ss[0, 3:4] = jnp.sum(wtr[1] * wtr[1], axis=0, keepdims=True)
    for copy in c_copies:
        copy.wait()
    total_valid = cnt[0, 0:1, 0:1]
    for d in range(1, nz):
        total_valid = total_valid + cnt[d, 0:1, 0:1]

    w_copies = []
    for m in range(3):
        for copy in g_copies[m * (nz - 1):(m + 1) * (nz - 1)]:
            copy.wait()
        grad = gfull[m, here, :]
        for d in range(1, nz):
            grad = grad + grecv[d - 1, m].astype(F32)
        old = wtr[m, here, :]
        raised = old + grad / total_valid
        if m == 2:
            rescale = jnp.sqrt(jnp.sum(old * old, -1, keepdims=True) + 1e-06) / jnp.sqrt(
                jnp.sum(raised * raised, -1, keepdims=True) + 1e-06
            )
            raised = raised * rescale
        else:
            ss[0, m:m + 1] = jnp.sum(raised * raised, axis=0, keepdims=True)
        news[0, m] = raised.astype(BF16)
        for d in range(1, nz):
            w_copies.append(send(news.at[0, m], news.at[d, m], "view", view_peer(d)))
        if m == 1:
            ss_copies = [send(ss.at[0], ss.at[d], "row", flip(me, d)) for d in range(1, nr)]
    for copy in ss_copies:
        copy.wait()
    strip_sums = ss[0]
    for d in range(1, nr):
        strip_sums = strip_sums + ss[d]
    ssz[0] = strip_sums[0:2]
    ssz_copies = [send(ssz.at[0], ssz.at[d], "view", view_peer(d)) for d in range(1, nz)]
    for copy in ssz_copies:
        copy.wait()
    new_sums = ssz[0]
    for d in range(1, nz):
        new_sums = new_sums + ssz[d]
    scales = jnp.sqrt(strip_sums[2:4] + 1e-06) / jnp.sqrt(new_sums + 1e-06)

    for copy in w_copies:
        copy.wait()
    new_first, new_third, new_second = (
        jnp.concatenate([news[d, m] for d in range(nz)], axis=0) for m in range(3)
    )

    def share(d):
        keys = kall[d].astype(F32)
        first = dot((keys * scales[0:1]).astype(BF16), new_first, NT)
        third = dot((keys * scales[1:2]).astype(BF16), new_third, NT)
        return dot((first * jax.nn.sigmoid(first) * third).astype(BF16), new_second)

    o_copies = {}
    for d in list(range(3, nr, 2)) + list(range(2, nr, 2)) + [1, 0]:
        total = share(d)
        if d == 0:
            continue
        if d % 2 == 0:
            o_copies[d + 1].wait_recv()
            total = total + orecv[d].astype(F32)
        osend[d - 1] = total.astype(BF16)
        o_copies[d] = send(
            osend.at[d - 1], orecv.at[d - 1], "row", flip(me, 1) if d % 2 else flip(me, d)
        )
    for d in [1] + list(range(2, nr, 2)):
        o_copies[d].wait_recv()
        total = total + orecv[d - 1].astype(F32)
    out_ref[...] = total.astype(BF16)
    for copies in (s_copies, k_copies, o_copies):
        settle(copies)


def fused_step(
    nr, nz,
    query_feats, key_feats, value_feats, target, token_rates, row_reach, view_counts,
    w_first, w_third, w_second,
):
    _, row_count, cols, width = query_feats.shape
    tokens = row_count * cols
    hid = width // nr
    part = hid // nz
    edge = HALO * cols
    copies = 4 + 4 * (nr - 1) + 8 * (nz - 1)
    smem = pl.BlockSpec(memory_space=pltpu.SMEM)
    anywhere = pl.BlockSpec(memory_space=pl.ANY)
    flat = lambda a: a.reshape(tokens, width)
    out = pl.pallas_call(
        functools.partial(step_kernel, nr, nz, cols),
        out_shape=jax.ShapeDtypeStruct((tokens, width), BF16),
        in_specs=[anywhere] * 5 + [smem] * 2 + [anywhere] * 3,
        out_specs=pl.BlockSpec(memory_space=pltpu.VMEM),
        scratch_shapes=[
            pltpu.VMEM((tokens, width), BF16),
            pltpu.VMEM((tokens, width), BF16),
            pltpu.VMEM((tokens, width), BF16),
            pltpu.VMEM((tokens, width), BF16),
            pltpu.VMEM((1, tokens), F32),
            pltpu.VMEM((width, hid), BF16),
            pltpu.VMEM((width, hid), BF16),
            pltpu.VMEM((hid, width), BF16),
            pltpu.VMEM((2, 2 * edge, width), BF16),
            pltpu.VMEM((nr, tokens, width), BF16),
            pltpu.VMEM((nr, tokens, width), BF16),
            pltpu.VMEM((nz, 8, 128), F32),
            pltpu.VMEM((3, hid, width), F32),
            pltpu.VMEM((nz, 3, part, width), BF16),
            pltpu.VMEM((nz - 1, 3, part, width), BF16),
            pltpu.VMEM((3, hid, width), F32),
            pltpu.VMEM((nz, 3, part, width), BF16),
            pltpu.VMEM((nr, 4, width), F32),
            pltpu.VMEM((nz, 2, width), F32),
            pltpu.VMEM((nr - 1, tokens, width), BF16),
            pltpu.VMEM((nr - 1, tokens, width), BF16),
            pltpu.SemaphoreType.DMA((8,)),
            pltpu.SemaphoreType.DMA((copies,)),
            pltpu.SemaphoreType.DMA((copies,)),
        ],
        compiler_params=pltpu.CompilerParams(collective_id=0, has_side_effects=True),
    )(
        flat(query_feats), flat(key_feats), flat(value_feats), flat(target),
        token_rates.reshape(1, tokens), row_reach, view_counts,
        w_first.reshape(width, width), w_third.reshape(width, width), w_second.reshape(width, width),
    )
    return out.reshape(query_feats.shape)


def solution(mesh):
    placed = (
        P("view", "row", None, "head"),
        P("view", "row", None, "head"),
        P("view", "row", None, "head"),
        P("view", "row", None, "head"),
        P("view", "head", "row"),
        P("row"),
        P("view"),
        P("head", None, None),
        P("head", None, None),
        P("head", None, None),
    )
    nr, nz = mesh.shape["row"], mesh.shape["view"]
    pairs = nr > 1 and nr & (nr - 1) == 0
    fits = pairs and nz > 1 and HD % (128 * nr) == 0 and HD % (16 * nr * nz) == 0
    return jax.shard_map(
        functools.partial(fused_step, nr, nz) if fits else per_device,
        mesh=mesh,
        in_specs=placed,
        out_specs=P("view", "row", None, "head"),
        check_vma=False,
    )
```

```python
import functools
import math

import jax
import jax.numpy as jnp
from jax import lax
from jax.experimental import pallas as pl
from jax.experimental.pallas import tpu as pltpu
from jax.sharding import PartitionSpec as P

HD = 512
ATT_HD = 128
HALO = 2
MESH = pl.DeviceIdType.MESH
BF16 = jnp.bfloat16
F32 = jnp.float32
NT = (((1,), (1,)), ((), ()))
TN = (((0,), (0,)), ((), ()))


def with_halo(value, sides, width):
    for axis, dim in sides:
        size, length = (lax.axis_size(axis), value.shape[dim])
        up = [(i, (i + 1) % size) for i in range(size - 1)]
        down = [(j, i) for i, j in up]
        last = lax.slice_in_dim(value, length - width, length, axis=dim)
        leading = lax.slice_in_dim(value, 0, width, axis=dim)
        before = lax.ppermute(last, axis, up)
        after = lax.ppermute(leading, axis, down)
        value = jnp.concatenate([before, value, after], axis=dim)
    return value


def silu_slope(values_in):
    sigmoid_x = jax.nn.sigmoid(values_in)
    return sigmoid_x * (1.0 + values_in * (1.0 - sigmoid_x))


def attend(
    query_rows,
    key_rows,
    value_rows,
    q_row_ids,
    k_row_ids,
    q_tok,
    k_tok,
    k_valid,
    q_reach,
    grid_rows,
):
    count_q = query_rows.shape[0]
    count_k = key_rows.shape[0]
    groups = query_rows.shape[1] // ATT_HD
    query_heads = query_rows.reshape(count_q, groups, ATT_HD)
    key_heads = key_rows.reshape(count_k, groups, ATT_HD)
    value_heads = value_rows.reshape(count_k, groups, ATT_HD)
    scores = jnp.einsum(
        "qhd,khd->hqk", query_heads, key_heads, preferred_element_type=jnp.float32
    ) / math.sqrt(ATT_HD)
    inside = (k_row_ids >= 0) & (k_row_ids < grid_rows)
    in_band = jnp.abs(k_row_ids[None, :] - q_row_ids[:, None]) <= q_reach[:, None]
    allowed = in_band & inside[None, :] & (k_valid[None, :] | (k_tok[None, :] == q_tok[:, None]))
    scores = jnp.where(allowed[None], scores, -1e30)
    row_top = jnp.max(scores, -1, keepdims=True)
    powers = jnp.exp(scores - row_top)
    weights = (powers / jnp.sum(powers, -1, keepdims=True)).astype(jnp.bfloat16)
    output_rows = jnp.einsum(
        "hqk,khd->qhd", weights, value_heads, preferred_element_type=jnp.float32
    )
    return output_rows.reshape(count_q, groups * ATT_HD).astype(jnp.bfloat16)


def renorm(old_matrix, grad, total_valid):
    old_rows = old_matrix.astype(jnp.float32)
    raised = old_rows + grad / total_valid
    rescale = jnp.sqrt(jnp.sum(old_rows * old_rows, -1, keepdims=True) + 1e-06) / jnp.sqrt(
        jnp.sum(raised * raised, -1, keepdims=True) + 1e-06
    )
    return (raised * rescale).astype(jnp.bfloat16)


def per_device(
    query_feats,
    key_feats,
    value_feats,
    target,
    token_rates,
    row_reach,
    view_counts,
    w_first,
    w_third,
    w_second,
):
    row_count = query_feats.shape[1]
    col_count = query_feats.shape[2]
    feat_width = query_feats.shape[3]
    heads_here = feat_width // HD
    tokens_here = row_count * col_count
    key_span = row_count + 2 * HALO
    grid_rows = lax.axis_size("row") * row_count
    row_base = lax.axis_index("row") * row_count
    view_total = view_counts[0]
    total_valid = lax.psum(view_total.astype(jnp.float32), "view")
    paired = jnp.stack([key_feats[0], value_feats[0]], 0)
    padded = with_halo(paired, (("row", 1),), HALO)
    q_row_ids = row_base + jnp.repeat(jnp.arange(row_count, dtype=jnp.int32), col_count)
    k_row_ids = row_base - HALO + jnp.repeat(jnp.arange(key_span, dtype=jnp.int32), col_count)
    q_tok = q_row_ids * col_count + jnp.tile(jnp.arange(col_count, dtype=jnp.int32), row_count)
    k_tok = k_row_ids * col_count + jnp.tile(jnp.arange(col_count, dtype=jnp.int32), key_span)
    k_valid = k_tok < view_total
    q_reach = jnp.repeat(row_reach, col_count)
    attended = attend(
        query_feats[0].reshape(tokens_here, feat_width),
        padded[0].reshape(key_span * col_count, feat_width),
        padded[1].reshape(key_span * col_count, feat_width),
        q_row_ids,
        k_row_ids,
        q_tok,
        k_tok,
        k_valid,
        q_reach,
        grid_rows,
    )
    attended = attended.reshape(tokens_here, heads_here, HD).astype(jnp.float32)
    fast_keys = (
        attended * lax.rsqrt(jnp.mean(attended * attended, -1, keepdims=True) + 1e-06)
    ).astype(jnp.bfloat16)
    valid_mask = (q_tok < view_total).astype(jnp.float32)
    rates_tok = token_rates[0].T
    scaled = (
        rates_tok[:, :, None]
        * valid_mask[:, None, None]
        * target[0].reshape(tokens_here, heads_here, HD).astype(jnp.float32)
    ).astype(jnp.bfloat16)
    first_proj = jnp.einsum("thi,hij->thj", fast_keys, w_first, preferred_element_type=jnp.float32)
    third_proj = jnp.einsum("thi,hij->thj", fast_keys, w_third, preferred_element_type=jnp.float32)
    gated_rows = (jax.nn.silu(first_proj) * third_proj).astype(jnp.bfloat16)
    back_rows = jnp.einsum("tho,hjo->thj", scaled, w_second, preferred_element_type=jnp.float32)
    back_first = (back_rows * third_proj * silu_slope(first_proj)).astype(jnp.bfloat16)
    back_third = (back_rows * jax.nn.silu(first_proj)).astype(jnp.bfloat16)
    grad_first = jnp.einsum(
        "thi,thj->hij", fast_keys, back_first, preferred_element_type=jnp.float32
    )
    grad_third = jnp.einsum(
        "thi,thj->hij", fast_keys, back_third, preferred_element_type=jnp.float32
    )
    grad_second = jnp.einsum("thj,tho->hjo", gated_rows, scaled, preferred_element_type=jnp.float32)
    grad_first, grad_third, grad_second = lax.psum(
        (grad_first, grad_third, grad_second), ("view", "row")
    )
    new_first = renorm(w_first, grad_first, total_valid)
    new_third = renorm(w_third, grad_third, total_valid)
    new_second = renorm(w_second, grad_second, total_valid)
    applied = (
        jax.nn.silu(
            jnp.einsum("thi,hij->thj", fast_keys, new_first, preferred_element_type=jnp.float32)
        )
        * jnp.einsum("thi,hij->thj", fast_keys, new_third, preferred_element_type=jnp.float32)
    ).astype(jnp.bfloat16)
    fast_out = jnp.einsum(
        "thj,hjo->tho", applied, new_second, preferred_element_type=jnp.float32
    ).astype(jnp.bfloat16)
    return fast_out.reshape(1, row_count, col_count, feat_width)


def halve(values_in, size):
    if size & (size - 1) == 0:
        return values_in >> (size.bit_length() - 1)
    return lax.div(values_in, jnp.int32(size))


def dot(left, right, dims=(((1,), (0,)), ((), ()))):
    return lax.dot_general(left, right, dims, preferred_element_type=F32)


def flip(index, bits):
    bit = 1
    while bit <= bits:
        if bits & bit:
            index = index + bit - 2 * bit * lax.rem(lax.div(index, bit), 2)
        bit *= 2
    return index


def step_kernel(
    nr, nz, cols,
    q_hbm, k_hbm, v_hbm, t_hbm, rates_hbm, reach_hbm, count_hbm, wf_hbm, wt_hbm, ws_hbm,
    out_ref,
    q_ref, k_ref, v_ref, t_ref, rates_ref, reach_ref, count_ref, wf, wt, ws, halo, raw, kall, sall, cnt, gfull, gsend, grecv,
    wtr, news, ss, ssz, osend, orecv, load_sem, send_sem, recv_sem,
):
    tokens, width = q_ref.shape
    rows_here = tokens // cols
    hid = width // nr
    part = hid // nz
    edge = HALO * cols
    heads = width // ATT_HD
    me = lax.axis_index("row")
    mz = lax.axis_index("view")
    mine = pl.ds(pl.multiple_of(me * hid, hid), hid)
    here = pl.ds(pl.multiple_of(mz * part, part), part)

    def view_peer(shift):
        return lax.rem(mz + (shift + nz), nz)

    barrier = pltpu.get_barrier_semaphore()
    for d in range(1, nr):
        pl.semaphore_signal(barrier, inc=1, device_id={"row": flip(me, d)}, device_id_type=MESH)
    for d in range(1, nz):
        pl.semaphore_signal(barrier, inc=1, device_id={"view": view_peer(d)}, device_id_type=MESH)
    loads = [
        pltpu.make_async_copy(source, target, load_sem.at[i])
        for i, (source, target) in enumerate((
            (count_hbm, count_ref), (reach_hbm, reach_ref), (k_hbm, k_ref), (v_hbm, v_ref),
            (t_hbm, t_ref), (rates_hbm, rates_ref), (q_hbm, q_ref),
            (wf_hbm.at[:, mine], wf), (wt_hbm.at[:, mine], wt), (ws_hbm.at[mine, :], ws),
        ))
    ]
    for load in loads:
        load.start()

    used = [0]

    def send(source, target, axis, peer):
        slot = used[0]
        used[0] += 1
        copy = pltpu.make_async_remote_copy(
            src_ref=source, dst_ref=target,
            send_sem=send_sem.at[slot], recv_sem=recv_sem.at[slot],
            device_id={axis: peer}, device_id_type=MESH,
        )
        copy.start()
        return copy

    straight = [1] + list(range(2, nr, 2))

    def spread(at):
        return {d: send(at(0), at(d), "row", flip(me, d)) for d in straight}

    def hand_on(at, copies):
        for d in range(2, nr, 2):
            copies[d].wait_recv()
            copies[d + 1] = send(at(d), at(d + 1), "row", flip(me, 1))

    def settle(copies):
        for d in copies:
            copies[d].wait_send()

    above = lax.rem(me + 1, nr)
    below = lax.rem(me + (nr - 1), nr)

    row_base = me * rows_here
    tok_base = me * tokens
    for load in loads[:2]:
        load.wait()
    view_total = count_ref[0]
    cnt[0] = jnp.full((8, 128), view_total, jnp.int32).astype(F32)
    sub = lax.broadcasted_iota(jnp.int32, (tokens, tokens), 0)
    lane = lax.broadcasted_iota(jnp.int32, (tokens, tokens), 1)
    tok_col = tok_base + lax.broadcasted_iota(jnp.int32, (tokens, 1), 0)
    valid_col = (tok_col < view_total).astype(F32)
    for load in loads[2:6]:
        load.wait()
    rate_col = jnp.sum(jnp.where(sub == lane, rates_ref[...], 0.0), axis=1, keepdims=True)
    sall[0] = (rate_col * valid_col * t_ref[...].astype(F32)).astype(BF16)

    def allowed(q_tok, k_tok):
        q_row = halve(q_tok, cols)
        k_row = halve(k_tok + edge, cols) - HALO
        reach = jnp.zeros(q_tok.shape, jnp.int32)
        for r in range(rows_here):
            reach = jnp.where(q_row == r, reach_ref[r], reach)
        k_abs = k_row + row_base
        return (
            (jnp.abs(k_row - q_row) <= reach)
            & (k_abs >= 0)
            & (k_abs < nr * rows_here)
            & ((k_tok + tok_base < view_total) | (k_tok == q_tok))
        )

    near_ok = allowed(sub, lane)
    far_q = lax.broadcasted_iota(jnp.int32, (tokens, 2 * edge), 0)
    far_k = lax.broadcasted_iota(jnp.int32, (tokens, 2 * edge), 1)
    far_ok = allowed(far_q, jnp.where(far_k < edge, far_k - edge, far_k - edge + tokens))
    root = 1.0 / math.sqrt(ATT_HD)
    spans = [slice(h * ATT_HD, (h + 1) * ATT_HD) for h in range(heads)]
    loads[6].wait()
    near = [
        jnp.where(near_ok, dot(q_ref[:, hs], k_ref[:, hs], NT) * root, -1e30) for hs in spans
    ]
    near_top = [jnp.max(scores, axis=-1, keepdims=True) for scores in near]

    pl.semaphore_wait(barrier, (nr - 1) + (nz - 1))

    halo_copies = []
    for i, ref in enumerate((k_ref, v_ref)):
        halo_copies.append(send(ref.at[pl.ds(tokens - edge, edge)], halo.at[i, pl.ds(0, edge)], "row", above))
        halo_copies.append(send(ref.at[pl.ds(0, edge)], halo.at[i, pl.ds(edge, edge)], "row", below))
    s_copies = spread(lambda d: sall.at[d])
    c_copies = [send(cnt.at[0], cnt.at[d], "view", view_peer(d)) for d in range(1, nz)]
    for load in loads[7:]:
        load.wait()
    wtr[0] = wf[...].astype(F32).T
    wtr[1] = wt[...].astype(F32).T
    wtr[2] = ws[...].astype(F32)
    for copy in halo_copies:
        copy.wait()
    k_copies = []
    for h, hs in enumerate(spans):
        far = jnp.where(far_ok, dot(q_ref[:, hs], halo[0, :, hs], NT) * root, -1e30)
        top = jnp.maximum(near_top[h], jnp.max(far, axis=-1, keepdims=True))
        near_pow = jnp.exp(near[h] - top)
        far_pow = jnp.exp(far - top)
        inverse = 1.0 / (
            jnp.sum(near_pow, axis=-1, keepdims=True) + jnp.sum(far_pow, axis=-1, keepdims=True)
        )
        piece = dot((near_pow * inverse).astype(BF16), v_ref[:, hs]) + dot(
            (far_pow * inverse).astype(BF16), halo[1, :, hs]
        )
        raw[0, h] = piece.astype(BF16)
        k_copies.append(spread(lambda d, h=h: raw.at[d, h]))
    hand_on(lambda d: sall.at[d], s_copies)

    def normalise(d):
        pieces = [raw[d, h].astype(F32) for h in range(heads)]
        total_sq = jnp.sum(pieces[0] * pieces[0], axis=-1, keepdims=True)
        for piece in pieces[1:]:
            total_sq = total_sq + jnp.sum(piece * piece, axis=-1, keepdims=True)
        norm = lax.rsqrt(total_sq * (1.0 / width) + 1e-06)
        for hs, piece in zip(spans, pieces):
            kall[d, :, hs] = (piece * norm).astype(BF16)

    def factors(d):
        normalise(d)
        first = dot(kall[d], wf[...])
        third = dot(kall[d], wt[...])
        back = dot(sall[d], ws[...], NT)
        sig = jax.nn.sigmoid(first)
        gate = first * sig
        return (
            ((back * third * (sig * (1.0 + first * (1.0 - sig)))).astype(BF16), kall),
            ((back * gate).astype(BF16), kall),
            ((gate * third).astype(BF16), sall),
        )

    order = [0] + straight + list(range(3, nr, 2))
    g_copies = []
    for d in order:
        if d == 2:
            for h in range(heads):
                hand_on(lambda e, h=h: raw.at[e, h], k_copies[h])
        if d % 2:
            for copies in k_copies + [s_copies]:
                copies[d].wait_recv()
        for m, (left, right) in enumerate(factors(d)):
            grad = dot(left, right[d], TN)
            if d:
                grad = gfull[m] + grad
            gfull[m] = grad
            if d == order[-1]:
                for z in range(nz):
                    gsend[z, m] = grad[z * part:(z + 1) * part].astype(BF16)
                for e in range(1, nz):
                    g_copies.append(
                        send(gsend.at[view_peer(e), m], grecv.at[e - 1, m], "view", view_peer(e))
                    )
    ss[0, 2:3] = jnp.sum(wtr[0] * wtr[0], axis=0, keepdims=True)
    ss[0, 3:4] = jnp.sum(wtr[1] * wtr[1], axis=0, keepdims=True)
    for copy in c_copies:
        copy.wait()
    total_valid = cnt[0, 0:1, 0:1]
    for d in range(1, nz):
        total_valid = total_valid + cnt[d, 0:1, 0:1]

    w_copies = []
    for m in range(3):
        for copy in g_copies[m * (nz - 1):(m + 1) * (nz - 1)]:
            copy.wait()
        grad = gfull[m, here, :]
        for d in range(1, nz):
            grad = grad + grecv[d - 1, m].astype(F32)
        old = wtr[m, here, :]
        raised = old + grad / total_valid
        if m == 2:
            rescale = jnp.sqrt(jnp.sum(old * old, -1, keepdims=True) + 1e-06) / jnp.sqrt(
                jnp.sum(raised * raised, -1, keepdims=True) + 1e-06
            )
            raised = raised * rescale
        else:
            ss[0, m:m + 1] = jnp.sum(raised * raised, axis=0, keepdims=True)
        news[0, m] = raised.astype(BF16)
        for d in range(1, nz):
            w_copies.append(send(news.at[0, m], news.at[d, m], "view", view_peer(d)))
        if m == 1:
            ss_copies = [send(ss.at[0], ss.at[d], "row", flip(me, d)) for d in range(1, nr)]
    for copy in ss_copies:
        copy.wait()
    strip_sums = ss[0]
    for d in range(1, nr):
        strip_sums = strip_sums + ss[d]
    ssz[0] = strip_sums[0:2]
    ssz_copies = [send(ssz.at[0], ssz.at[d], "view", view_peer(d)) for d in range(1, nz)]
    for copy in ssz_copies:
        copy.wait()
    new_sums = ssz[0]
    for d in range(1, nz):
        new_sums = new_sums + ssz[d]
    scales = jnp.sqrt(strip_sums[2:4] + 1e-06) / jnp.sqrt(new_sums + 1e-06)

    for copy in w_copies:
        copy.wait()
    new_first, new_third, new_second = (
        jnp.concatenate([news[d, m] for d in range(nz)], axis=0) for m in range(3)
    )

    def share(d):
        keys = kall[d].astype(F32)
        first = dot((keys * scales[0:1]).astype(BF16), new_first, NT)
        third = dot((keys * scales[1:2]).astype(BF16), new_third, NT)
        return dot((first * jax.nn.sigmoid(first) * third).astype(BF16), new_second)

    o_copies = {}
    for d in list(range(3, nr, 2)) + list(range(2, nr, 2)) + [1, 0]:
        total = share(d)
        if d == 0:
            continue
        if d % 2 == 0:
            o_copies[d + 1].wait_recv()
            total = total + orecv[d].astype(F32)
        osend[d - 1] = total.astype(BF16)
        o_copies[d] = send(
            osend.at[d - 1], orecv.at[d - 1], "row", flip(me, 1) if d % 2 else flip(me, d)
        )
    for d in [1] + list(range(2, nr, 2)):
        o_copies[d].wait_recv()
        total = total + orecv[d - 1].astype(F32)
    out_ref[...] = total.astype(BF16)
    for copies in k_copies + [s_copies, o_copies]:
        settle(copies)


def fused_step(
    nr, nz,
    query_feats, key_feats, value_feats, target, token_rates, row_reach, view_counts,
    w_first, w_third, w_second,
):
    _, row_count, cols, width = query_feats.shape
    tokens = row_count * cols
    hid = width // nr
    part = hid // nz
    edge = HALO * cols
    heads = width // ATT_HD
    copies = 4 + (3 + heads) * (nr - 1) + 8 * (nz - 1)
    anywhere = pl.BlockSpec(memory_space=pl.ANY)
    flat = lambda a: a.reshape(tokens, width)
    out = pl.pallas_call(
        functools.partial(step_kernel, nr, nz, cols),
        out_shape=pltpu.VMEM((tokens, width), BF16),
        in_specs=[anywhere] * 5 + [pl.BlockSpec(memory_space=pltpu.HBM)] * 2 + [anywhere] * 3,
        out_specs=pl.BlockSpec(memory_space=pltpu.VMEM),
        scratch_shapes=[
            pltpu.VMEM((tokens, width), BF16),
            pltpu.VMEM((tokens, width), BF16),
            pltpu.VMEM((tokens, width), BF16),
            pltpu.VMEM((tokens, width), BF16),
            pltpu.VMEM((1, tokens), F32),
            pltpu.SMEM((row_count,), jnp.int32),
            pltpu.SMEM((1,), jnp.int32),
            pltpu.VMEM((width, hid), BF16),
            pltpu.VMEM((width, hid), BF16),
            pltpu.VMEM((hid, width), BF16),
            pltpu.VMEM((2, 2 * edge, width), BF16),
            pltpu.VMEM((nr, heads, tokens, ATT_HD), BF16),
            pltpu.VMEM((nr, tokens, width), BF16),
            pltpu.VMEM((nr, tokens, width), BF16),
            pltpu.VMEM((nz, 8, 128), F32),
            pltpu.VMEM((3, hid, width), F32),
            pltpu.VMEM((nz, 3, part, width), BF16),
            pltpu.VMEM((nz - 1, 3, part, width), BF16),
            pltpu.VMEM((3, hid, width), F32),
            pltpu.VMEM((nz, 3, part, width), BF16),
            pltpu.VMEM((nr, 4, width), F32),
            pltpu.VMEM((nz, 2, width), F32),
            pltpu.VMEM((nr - 1, tokens, width), BF16),
            pltpu.VMEM((nr - 1, tokens, width), BF16),
            pltpu.SemaphoreType.DMA((10,)),
            pltpu.SemaphoreType.DMA((copies,)),
            pltpu.SemaphoreType.DMA((copies,)),
        ],
        compiler_params=pltpu.CompilerParams(collective_id=0, has_side_effects=True),
    )(
        flat(query_feats), flat(key_feats), flat(value_feats), flat(target),
        token_rates.reshape(1, tokens), row_reach, view_counts,
        w_first.reshape(width, width), w_third.reshape(width, width), w_second.reshape(width, width),
    )
    return out.reshape(query_feats.shape)


def solution(mesh):
    placed = (
        P("view", "row", None, "head"),
        P("view", "row", None, "head"),
        P("view", "row", None, "head"),
        P("view", "row", None, "head"),
        P("view", "head", "row"),
        P("row"),
        P("view"),
        P("head", None, None),
        P("head", None, None),
        P("head", None, None),
    )
    nr, nz = mesh.shape["row"], mesh.shape["view"]
    pairs = nr > 1 and nr & (nr - 1) == 0
    fits = pairs and nz > 1 and HD % (128 * nr) == 0 and HD % (16 * nr * nz) == 0
    return jax.shard_map(
        functools.partial(fused_step, nr, nz) if fits else per_device,
        mesh=mesh,
        in_specs=placed,
        out_specs=P("view", "row", None, "head"),
        check_vma=False,
    )
```

```python
import functools
import math

import jax
import jax.numpy as jnp
from jax import lax
from jax.experimental import pallas as pl
from jax.experimental.pallas import tpu as pltpu
from jax.sharding import PartitionSpec as P

HD = 512
ATT_HD = 128
HALO = 2
MESH = pl.DeviceIdType.MESH
BF16 = jnp.bfloat16
F32 = jnp.float32
NT = (((1,), (1,)), ((), ()))
TN = (((0,), (0,)), ((), ()))


def with_halo(value, sides, width):
    for axis, dim in sides:
        size, length = (lax.axis_size(axis), value.shape[dim])
        up = [(i, (i + 1) % size) for i in range(size - 1)]
        down = [(j, i) for i, j in up]
        last = lax.slice_in_dim(value, length - width, length, axis=dim)
        leading = lax.slice_in_dim(value, 0, width, axis=dim)
        before = lax.ppermute(last, axis, up)
        after = lax.ppermute(leading, axis, down)
        value = jnp.concatenate([before, value, after], axis=dim)
    return value


def silu_slope(values_in):
    sigmoid_x = jax.nn.sigmoid(values_in)
    return sigmoid_x * (1.0 + values_in * (1.0 - sigmoid_x))


def attend(
    query_rows,
    key_rows,
    value_rows,
    q_row_ids,
    k_row_ids,
    q_tok,
    k_tok,
    k_valid,
    q_reach,
    grid_rows,
):
    count_q = query_rows.shape[0]
    count_k = key_rows.shape[0]
    groups = query_rows.shape[1] // ATT_HD
    query_heads = query_rows.reshape(count_q, groups, ATT_HD)
    key_heads = key_rows.reshape(count_k, groups, ATT_HD)
    value_heads = value_rows.reshape(count_k, groups, ATT_HD)
    scores = jnp.einsum(
        "qhd,khd->hqk", query_heads, key_heads, preferred_element_type=jnp.float32
    ) / math.sqrt(ATT_HD)
    inside = (k_row_ids >= 0) & (k_row_ids < grid_rows)
    in_band = jnp.abs(k_row_ids[None, :] - q_row_ids[:, None]) <= q_reach[:, None]
    allowed = in_band & inside[None, :] & (k_valid[None, :] | (k_tok[None, :] == q_tok[:, None]))
    scores = jnp.where(allowed[None], scores, -1e30)
    row_top = jnp.max(scores, -1, keepdims=True)
    powers = jnp.exp(scores - row_top)
    weights = (powers / jnp.sum(powers, -1, keepdims=True)).astype(jnp.bfloat16)
    output_rows = jnp.einsum(
        "hqk,khd->qhd", weights, value_heads, preferred_element_type=jnp.float32
    )
    return output_rows.reshape(count_q, groups * ATT_HD).astype(jnp.bfloat16)


def renorm(old_matrix, grad, total_valid):
    old_rows = old_matrix.astype(jnp.float32)
    raised = old_rows + grad / total_valid
    rescale = jnp.sqrt(jnp.sum(old_rows * old_rows, -1, keepdims=True) + 1e-06) / jnp.sqrt(
        jnp.sum(raised * raised, -1, keepdims=True) + 1e-06
    )
    return (raised * rescale).astype(jnp.bfloat16)


def per_device(
    query_feats,
    key_feats,
    value_feats,
    target,
    token_rates,
    row_reach,
    view_counts,
    w_first,
    w_third,
    w_second,
):
    row_count = query_feats.shape[1]
    col_count = query_feats.shape[2]
    feat_width = query_feats.shape[3]
    heads_here = feat_width // HD
    tokens_here = row_count * col_count
    key_span = row_count + 2 * HALO
    grid_rows = lax.axis_size("row") * row_count
    row_base = lax.axis_index("row") * row_count
    view_total = view_counts[0]
    total_valid = lax.psum(view_total.astype(jnp.float32), "view")
    paired = jnp.stack([key_feats[0], value_feats[0]], 0)
    padded = with_halo(paired, (("row", 1),), HALO)
    q_row_ids = row_base + jnp.repeat(jnp.arange(row_count, dtype=jnp.int32), col_count)
    k_row_ids = row_base - HALO + jnp.repeat(jnp.arange(key_span, dtype=jnp.int32), col_count)
    q_tok = q_row_ids * col_count + jnp.tile(jnp.arange(col_count, dtype=jnp.int32), row_count)
    k_tok = k_row_ids * col_count + jnp.tile(jnp.arange(col_count, dtype=jnp.int32), key_span)
    k_valid = k_tok < view_total
    q_reach = jnp.repeat(row_reach, col_count)
    attended = attend(
        query_feats[0].reshape(tokens_here, feat_width),
        padded[0].reshape(key_span * col_count, feat_width),
        padded[1].reshape(key_span * col_count, feat_width),
        q_row_ids,
        k_row_ids,
        q_tok,
        k_tok,
        k_valid,
        q_reach,
        grid_rows,
    )
    attended = attended.reshape(tokens_here, heads_here, HD).astype(jnp.float32)
    fast_keys = (
        attended * lax.rsqrt(jnp.mean(attended * attended, -1, keepdims=True) + 1e-06)
    ).astype(jnp.bfloat16)
    valid_mask = (q_tok < view_total).astype(jnp.float32)
    rates_tok = token_rates[0].T
    scaled = (
        rates_tok[:, :, None]
        * valid_mask[:, None, None]
        * target[0].reshape(tokens_here, heads_here, HD).astype(jnp.float32)
    ).astype(jnp.bfloat16)
    first_proj = jnp.einsum("thi,hij->thj", fast_keys, w_first, preferred_element_type=jnp.float32)
    third_proj = jnp.einsum("thi,hij->thj", fast_keys, w_third, preferred_element_type=jnp.float32)
    gated_rows = (jax.nn.silu(first_proj) * third_proj).astype(jnp.bfloat16)
    back_rows = jnp.einsum("tho,hjo->thj", scaled, w_second, preferred_element_type=jnp.float32)
    back_first = (back_rows * third_proj * silu_slope(first_proj)).astype(jnp.bfloat16)
    back_third = (back_rows * jax.nn.silu(first_proj)).astype(jnp.bfloat16)
    grad_first = jnp.einsum(
        "thi,thj->hij", fast_keys, back_first, preferred_element_type=jnp.float32
    )
    grad_third = jnp.einsum(
        "thi,thj->hij", fast_keys, back_third, preferred_element_type=jnp.float32
    )
    grad_second = jnp.einsum("thj,tho->hjo", gated_rows, scaled, preferred_element_type=jnp.float32)
    grad_first, grad_third, grad_second = lax.psum(
        (grad_first, grad_third, grad_second), ("view", "row")
    )
    new_first = renorm(w_first, grad_first, total_valid)
    new_third = renorm(w_third, grad_third, total_valid)
    new_second = renorm(w_second, grad_second, total_valid)
    applied = (
        jax.nn.silu(
            jnp.einsum("thi,hij->thj", fast_keys, new_first, preferred_element_type=jnp.float32)
        )
        * jnp.einsum("thi,hij->thj", fast_keys, new_third, preferred_element_type=jnp.float32)
    ).astype(jnp.bfloat16)
    fast_out = jnp.einsum(
        "thj,hjo->tho", applied, new_second, preferred_element_type=jnp.float32
    ).astype(jnp.bfloat16)
    return fast_out.reshape(1, row_count, col_count, feat_width)


def halve(values_in, size):
    if size & (size - 1) == 0:
        return values_in >> (size.bit_length() - 1)
    return lax.div(values_in, jnp.int32(size))


def dot(left, right, dims=(((1,), (0,)), ((), ()))):
    return lax.dot_general(left, right, dims, preferred_element_type=F32)


def flip(index, bits):
    bit = 1
    while bit <= bits:
        if bits & bit:
            index = index + bit - 2 * bit * lax.rem(lax.div(index, bit), 2)
        bit *= 2
    return index


def step_kernel(
    nr, nz, cols,
    q_hbm, k_hbm, v_hbm, t_hbm, rates_hbm, reach_hbm, count_hbm, wf_hbm, wt_hbm, ws_hbm,
    out_ref,
    q_ref, k_ref, v_ref, t_ref, rates_ref, reach_ref, count_ref, wf, wt, ws, halo, raw, kall, sall, cnt, gfull, gsend, grecv,
    wtr, news, ss, ssz, osend, orecv, load_sem, send_sem, recv_sem,
    wsend_sem, wrecv_sem,
):
    tokens, width = q_ref.shape
    rows_here = tokens // cols
    hid = width // nr
    part = hid // nz
    edge = HALO * cols
    heads = width // ATT_HD
    cuts = [0, part // 2] if part % 32 == 0 else [0]
    step = part // len(cuts)
    me = lax.axis_index("row")
    mz = lax.axis_index("view")
    mine = pl.ds(pl.multiple_of(me * hid, hid), hid)

    def view_peer(shift):
        return lax.rem(mz + (shift + nz), nz)

    barrier = pltpu.get_barrier_semaphore()
    for d in range(1, nr):
        pl.semaphore_signal(barrier, inc=1, device_id={"row": flip(me, d)}, device_id_type=MESH)
    for d in range(1, nz):
        pl.semaphore_signal(barrier, inc=1, device_id={"view": view_peer(d)}, device_id_type=MESH)
    loads = [
        pltpu.make_async_copy(source, target, load_sem.at[i])
        for i, (source, target) in enumerate((
            (count_hbm, count_ref), (reach_hbm, reach_ref), (k_hbm, k_ref), (v_hbm, v_ref),
            (t_hbm, t_ref), (rates_hbm, rates_ref), (q_hbm, q_ref),
            (wf_hbm.at[:, mine], wf), (wt_hbm.at[:, mine], wt), (ws_hbm.at[mine, :], ws),
        ))
    ]
    for load in loads:
        load.start()

    used = [0]

    def send(source, target, axis, peer):
        slot = used[0]
        used[0] += 1
        copy = pltpu.make_async_remote_copy(
            src_ref=source, dst_ref=target,
            send_sem=send_sem.at[slot], recv_sem=recv_sem.at[slot],
            device_id={axis: peer}, device_id_type=MESH,
        )
        copy.start()
        return copy

    straight = [1] + list(range(2, nr, 2))

    def spread(at):
        return {d: send(at(0), at(d), "row", flip(me, d)) for d in straight}

    def hand_on(at, copies):
        for d in range(2, nr, 2):
            copies[d].wait_recv()
            copies[d + 1] = send(at(d), at(d + 1), "row", flip(me, 1))

    def settle(copies):
        for d in copies:
            copies[d].wait_send()

    above = lax.rem(me + 1, nr)
    below = lax.rem(me + (nr - 1), nr)

    row_base = me * rows_here
    tok_base = me * tokens
    for load in loads[:2]:
        load.wait()
    view_total = count_ref[...]
    cnt[0] = jnp.broadcast_to(view_total.astype(F32), (8, 128))
    sub = lax.broadcasted_iota(jnp.int32, (tokens, tokens), 0)
    lane = lax.broadcasted_iota(jnp.int32, (tokens, tokens), 1)
    tok_col = tok_base + lax.broadcasted_iota(jnp.int32, (tokens, 1), 0)
    valid_col = (tok_col < view_total).astype(F32)
    for load in loads[2:6]:
        load.wait()
    rate_col = jnp.sum(jnp.where(sub == lane, rates_ref[...], 0.0), axis=1, keepdims=True)
    sall[0] = (rate_col * valid_col * t_ref[...].astype(F32)).astype(BF16)

    def allowed(q_tok, k_tok):
        q_row = halve(q_tok, cols)
        k_row = halve(k_tok + edge, cols) - HALO
        reach = jnp.zeros(q_tok.shape, jnp.int32)
        for r in range(rows_here):
            reach = jnp.where(q_row == r, reach_ref[r], reach)
        k_abs = k_row + row_base
        return (
            (jnp.abs(k_row - q_row) <= reach)
            & (k_abs >= 0)
            & (k_abs < nr * rows_here)
            & ((k_tok + tok_base < view_total) | (k_tok == q_tok))
        )

    near_ok = allowed(sub, lane)
    far_q = lax.broadcasted_iota(jnp.int32, (tokens, 2 * edge), 0)
    far_k = lax.broadcasted_iota(jnp.int32, (tokens, 2 * edge), 1)
    far_ok = allowed(far_q, jnp.where(far_k < edge, far_k - edge, far_k - edge + tokens))
    root = 1.0 / math.sqrt(ATT_HD)
    spans = [slice(h * ATT_HD, (h + 1) * ATT_HD) for h in range(heads)]
    loads[6].wait()
    near = [
        jnp.where(near_ok, dot(q_ref[:, hs], k_ref[:, hs], NT) * root, -1e30) for hs in spans
    ]
    near_top = [jnp.max(scores, axis=-1, keepdims=True) for scores in near]

    pl.semaphore_wait(barrier, (nr - 1) + (nz - 1))

    halo_copies = []
    for i, ref in enumerate((k_ref, v_ref)):
        halo_copies.append(send(ref.at[pl.ds(tokens - edge, edge)], halo.at[i, pl.ds(0, edge)], "row", above))
        halo_copies.append(send(ref.at[pl.ds(0, edge)], halo.at[i, pl.ds(edge, edge)], "row", below))
    s_copies = spread(lambda d: sall.at[d])
    c_copies = [send(cnt.at[0], cnt.at[d], "view", view_peer(d)) for d in range(1, nz)]
    for load in loads[7:]:
        load.wait()
    wtr[0] = wf[...].astype(F32).T
    wtr[1] = wt[...].astype(F32).T
    wtr[2] = ws[...].astype(F32)
    for copy in halo_copies:
        copy.wait()
    k_copies = []
    for h, hs in enumerate(spans):
        far = jnp.where(far_ok, dot(q_ref[:, hs], halo[0, :, hs], NT) * root, -1e30)
        top = jnp.maximum(near_top[h], jnp.max(far, axis=-1, keepdims=True))
        near_pow = jnp.exp(near[h] - top)
        far_pow = jnp.exp(far - top)
        inverse = 1.0 / (
            jnp.sum(near_pow, axis=-1, keepdims=True) + jnp.sum(far_pow, axis=-1, keepdims=True)
        )
        piece = dot((near_pow * inverse).astype(BF16), v_ref[:, hs]) + dot(
            (far_pow * inverse).astype(BF16), halo[1, :, hs]
        )
        raw[0, h] = piece.astype(BF16)
        k_copies.append(spread(lambda d, h=h: raw.at[d, h]))
    hand_on(lambda d: sall.at[d], s_copies)

    def normalise(d):
        pieces = [raw[d, h].astype(F32) for h in range(heads)]
        total_sq = jnp.sum(pieces[0] * pieces[0], axis=-1, keepdims=True)
        for piece in pieces[1:]:
            total_sq = total_sq + jnp.sum(piece * piece, axis=-1, keepdims=True)
        norm = lax.rsqrt(total_sq * (1.0 / width) + 1e-06)
        for hs, piece in zip(spans, pieces):
            kall[d, :, hs] = (piece * norm).astype(BF16)

    def factors(d):
        normalise(d)
        first = dot(kall[d], wf[...])
        third = dot(kall[d], wt[...])
        back = dot(sall[d], ws[...], NT)
        sig = jax.nn.sigmoid(first)
        gate = first * sig
        return (
            ((back * third * (sig * (1.0 + first * (1.0 - sig)))).astype(BF16), kall),
            ((back * gate).astype(BF16), kall),
            ((gate * third).astype(BF16), sall),
        )

    order = [0] + straight + list(range(3, nr, 2))
    g_copies = []
    for d in order:
        if d == 2:
            for h in range(heads):
                hand_on(lambda e, h=h: raw.at[e, h], k_copies[h])
        if d % 2:
            for copies in k_copies + [s_copies]:
                copies[d].wait_recv()
        for m, (left, right) in enumerate(factors(d)):
            grad = dot(left, right[d], TN)
            if d:
                grad = gfull[m] + grad
            gfull[m] = grad
            if d == order[-1]:
                for z in range(nz):
                    gsend[z, m] = grad[z * part:(z + 1) * part].astype(BF16)
                for off in cuts:
                    rows = pl.ds(off, step)
                    g_copies.append([
                        send(
                            gsend.at[view_peer(e), m, rows], grecv.at[e - 1, m, rows],
                            "view", view_peer(e),
                        )
                        for e in range(1, nz)
                    ])
    ss[0, 2:3] = jnp.sum(wtr[0] * wtr[0], axis=0, keepdims=True)
    ss[0, 3:4] = jnp.sum(wtr[1] * wtr[1], axis=0, keepdims=True)
    for copy in c_copies:
        copy.wait()
    total_valid = cnt[0, 0:1, 0:1]
    for d in range(1, nz):
        total_valid = total_valid + cnt[d, 0:1, 0:1]

    line = nz == 4
    side = lax.div(mz, 2)
    outer = lax.rem(mz, 3) == 0
    if line:
        partner = jnp.where(outer, 1 + side, 3 * side)
        targets = [2 - side, partner]
        sources = [2 - side, 3 - 3 * side, partner]
    else:
        targets = [view_peer(d) for d in range(1, nz)]
        sources = targets

    def weight_copy(chunk, source, to, way):
        m, off = divmod(chunk, len(cuts))
        spot = news.at[source, m, pl.ds(cuts[off], step)]
        return pltpu.make_async_remote_copy(
            src_ref=spot, dst_ref=spot,
            send_sem=wsend_sem.at[chunk, way], recv_sem=wrecv_sem.at[chunk, source],
            device_id={"view": to}, device_id_type=MESH,
        )

    def relay(chunk, ways):
        weight_copy(chunk, sources[ways], sources[ways], 0).wait_recv()
        if line and ways < 2:
            @pl.when(jnp.logical_not(outer))
            def _():
                weight_copy(chunk, sources[ways], partner, 2 + ways).start()

    def raise_chunk(chunk):
        m, off = divmod(chunk, len(cuts))
        off = cuts[off]
        for copy in g_copies[chunk]:
            copy.wait()
        rows = pl.ds(pl.multiple_of(mz * part + off, step), step)
        grad = gfull[m, rows, :]
        for d in range(1, nz):
            grad = grad + grecv[d - 1, m, off:off + step].astype(F32)
        old = wtr[m, rows, :]
        raised = old + grad / total_valid
        if m == 2:
            rescale = jnp.sqrt(jnp.sum(old * old, -1, keepdims=True) + 1e-06) / jnp.sqrt(
                jnp.sum(raised * raised, -1, keepdims=True) + 1e-06
            )
            raised = raised * rescale
        else:
            squares = jnp.sum(raised * raised, axis=0, keepdims=True)
            if off:
                squares = ss[0, m:m + 1] + squares
            ss[0, m:m + 1] = squares
        news[mz, m, off:off + step] = raised.astype(BF16)
        for way, to in enumerate(targets):
            weight_copy(chunk, mz, to, way).start()

    chunks = 3 * len(cuts)
    lag = 2 * len(cuts) - 1
    for chunk in range(chunks):
        raise_chunk(chunk)
        if chunk == 2 * len(cuts) - 1:
            ss_copies = [send(ss.at[0], ss.at[d], "row", flip(me, d)) for d in range(1, nr)]
        if chunk >= lag:
            for ways in range(len(sources)):
                relay(chunk - lag, ways)
    for copy in ss_copies:
        copy.wait()
    strip_sums = ss[0]
    for d in range(1, nr):
        strip_sums = strip_sums + ss[d]
    ssz[0] = strip_sums[0:2]
    ssz_copies = [send(ssz.at[0], ssz.at[d], "view", view_peer(d)) for d in range(1, nz)]
    for chunk in range(chunks - lag, chunks):
        for ways in range(len(sources)):
            relay(chunk, ways)
    for copy in ssz_copies:
        copy.wait()
    new_sums = ssz[0]
    for d in range(1, nz):
        new_sums = new_sums + ssz[d]
    scales = jnp.sqrt(strip_sums[2:4] + 1e-06) / jnp.sqrt(new_sums + 1e-06)

    new_first, new_third, new_second = (
        jnp.concatenate([news[d, m] for d in range(nz)], axis=0) for m in range(3)
    )

    def share(d):
        keys = kall[d].astype(F32)
        first = dot((keys * scales[0:1]).astype(BF16), new_first, NT)
        third = dot((keys * scales[1:2]).astype(BF16), new_third, NT)
        return dot((first * jax.nn.sigmoid(first) * third).astype(BF16), new_second)

    o_copies = {}
    for d in list(range(3, nr, 2)) + list(range(2, nr, 2)) + [1, 0]:
        total = share(d)
        if d == 0:
            continue
        if d % 2 == 0:
            o_copies[d + 1].wait_recv()
            total = total + orecv[d].astype(F32)
        osend[d - 1] = total.astype(BF16)
        o_copies[d] = send(
            osend.at[d - 1], orecv.at[d - 1], "row", flip(me, 1) if d % 2 else flip(me, d)
        )
    for d in [1] + list(range(2, nr, 2)):
        o_copies[d].wait_recv()
        total = total + orecv[d - 1].astype(F32)
    out_ref[...] = total.astype(BF16)
    for copies in k_copies + [s_copies, o_copies]:
        settle(copies)
    for chunk in range(chunks):
        for way, to in enumerate(targets):
            weight_copy(chunk, mz, to, way).wait_send()
    if line:
        @pl.when(jnp.logical_not(outer))
        def _():
            for chunk in range(chunks):
                for way in range(2):
                    weight_copy(chunk, sources[way], partner, 2 + way).wait_send()


def fused_step(
    nr, nz,
    query_feats, key_feats, value_feats, target, token_rates, row_reach, view_counts,
    w_first, w_third, w_second,
):
    _, row_count, cols, width = query_feats.shape
    tokens = row_count * cols
    hid = width // nr
    part = hid // nz
    edge = HALO * cols
    heads = width // ATT_HD
    cuts = 2 if part % 32 == 0 else 1
    copies = 4 + (3 + heads) * (nr - 1) + (2 + 3 * cuts) * (nz - 1)
    anywhere = pl.BlockSpec(memory_space=pl.ANY)
    flat = lambda a: a.reshape(tokens, width)
    out = pl.pallas_call(
        functools.partial(step_kernel, nr, nz, cols),
        out_shape=pltpu.VMEM((tokens, width), BF16),
        in_specs=[anywhere] * 5 + [pl.BlockSpec(memory_space=pltpu.HBM)] * 2 + [anywhere] * 3,
        out_specs=pl.BlockSpec(memory_space=pltpu.VMEM),
        scratch_shapes=[
            pltpu.VMEM((tokens, width), BF16),
            pltpu.VMEM((tokens, width), BF16),
            pltpu.VMEM((tokens, width), BF16),
            pltpu.VMEM((tokens, width), BF16),
            pltpu.VMEM((1, tokens), F32),
            pltpu.SMEM((row_count,), jnp.int32),
            pltpu.VMEM((1, 1), jnp.int32),
            pltpu.VMEM((width, hid), BF16),
            pltpu.VMEM((width, hid), BF16),
            pltpu.VMEM((hid, width), BF16),
            pltpu.VMEM((2, 2 * edge, width), BF16),
            pltpu.VMEM((nr, heads, tokens, ATT_HD), BF16),
            pltpu.VMEM((nr, tokens, width), BF16),
            pltpu.VMEM((nr, tokens, width), BF16),
            pltpu.VMEM((nz, 8, 128), F32),
            pltpu.VMEM((3, hid, width), F32),
            pltpu.VMEM((nz, 3, part, width), BF16),
            pltpu.VMEM((nz - 1, 3, part, width), BF16),
            pltpu.VMEM((3, hid, width), F32),
            pltpu.VMEM((nz, 3, part, width), BF16),
            pltpu.VMEM((nr, 4, width), F32),
            pltpu.VMEM((nz, 2, width), F32),
            pltpu.VMEM((nr - 1, tokens, width), BF16),
            pltpu.VMEM((nr - 1, tokens, width), BF16),
            pltpu.SemaphoreType.DMA((10,)),
            pltpu.SemaphoreType.DMA((copies,)),
            pltpu.SemaphoreType.DMA((copies,)),
            pltpu.SemaphoreType.DMA((3 * cuts, max(nz, 4))),
            pltpu.SemaphoreType.DMA((3 * cuts, nz)),
        ],
        compiler_params=pltpu.CompilerParams(collective_id=0, has_side_effects=True),
    )(
        flat(query_feats), flat(key_feats), flat(value_feats), flat(target),
        token_rates.reshape(1, tokens), row_reach, view_counts.reshape(1, 1),
        w_first.reshape(width, width), w_third.reshape(width, width), w_second.reshape(width, width),
    )
    return out.reshape(query_feats.shape)


def solution(mesh):
    placed = (
        P("view", "row", None, "head"),
        P("view", "row", None, "head"),
        P("view", "row", None, "head"),
        P("view", "row", None, "head"),
        P("view", "head", "row"),
        P("row"),
        P("view"),
        P("head", None, None),
        P("head", None, None),
        P("head", None, None),
    )
    nr, nz = mesh.shape["row"], mesh.shape["view"]
    pairs = nr > 1 and nr & (nr - 1) == 0
    fits = pairs and nz > 1 and HD % (128 * nr) == 0 and HD % (16 * nr * nz) == 0
    return jax.shard_map(
        functools.partial(fused_step, nr, nz) if fits else per_device,
        mesh=mesh,
        in_specs=placed,
        out_specs=P("view", "row", None, "head"),
        check_vma=False,
    )
```

```python
import functools
import math

import jax
import jax.numpy as jnp
from jax import lax
from jax.experimental import pallas as pl
from jax.experimental.pallas import tpu as pltpu
from jax.sharding import PartitionSpec as P

HD = 512
ATT_HD = 128
HALO = 2
MESH = pl.DeviceIdType.MESH
BF16 = jnp.bfloat16
F32 = jnp.float32
NT = (((1,), (1,)), ((), ()))
TN = (((0,), (0,)), ((), ()))


def with_halo(value, sides, width):
    for axis, dim in sides:
        size, length = (lax.axis_size(axis), value.shape[dim])
        up = [(i, (i + 1) % size) for i in range(size - 1)]
        down = [(j, i) for i, j in up]
        last = lax.slice_in_dim(value, length - width, length, axis=dim)
        leading = lax.slice_in_dim(value, 0, width, axis=dim)
        before = lax.ppermute(last, axis, up)
        after = lax.ppermute(leading, axis, down)
        value = jnp.concatenate([before, value, after], axis=dim)
    return value


def silu_slope(values_in):
    sigmoid_x = jax.nn.sigmoid(values_in)
    return sigmoid_x * (1.0 + values_in * (1.0 - sigmoid_x))


def attend(
    query_rows,
    key_rows,
    value_rows,
    q_row_ids,
    k_row_ids,
    q_tok,
    k_tok,
    k_valid,
    q_reach,
    grid_rows,
):
    count_q = query_rows.shape[0]
    count_k = key_rows.shape[0]
    groups = query_rows.shape[1] // ATT_HD
    query_heads = query_rows.reshape(count_q, groups, ATT_HD)
    key_heads = key_rows.reshape(count_k, groups, ATT_HD)
    value_heads = value_rows.reshape(count_k, groups, ATT_HD)
    scores = jnp.einsum(
        "qhd,khd->hqk", query_heads, key_heads, preferred_element_type=jnp.float32
    ) / math.sqrt(ATT_HD)
    inside = (k_row_ids >= 0) & (k_row_ids < grid_rows)
    in_band = jnp.abs(k_row_ids[None, :] - q_row_ids[:, None]) <= q_reach[:, None]
    allowed = in_band & inside[None, :] & (k_valid[None, :] | (k_tok[None, :] == q_tok[:, None]))
    scores = jnp.where(allowed[None], scores, -1e30)
    row_top = jnp.max(scores, -1, keepdims=True)
    powers = jnp.exp(scores - row_top)
    weights = (powers / jnp.sum(powers, -1, keepdims=True)).astype(jnp.bfloat16)
    output_rows = jnp.einsum(
        "hqk,khd->qhd", weights, value_heads, preferred_element_type=jnp.float32
    )
    return output_rows.reshape(count_q, groups * ATT_HD).astype(jnp.bfloat16)


def renorm(old_matrix, grad, total_valid):
    old_rows = old_matrix.astype(jnp.float32)
    raised = old_rows + grad / total_valid
    rescale = jnp.sqrt(jnp.sum(old_rows * old_rows, -1, keepdims=True) + 1e-06) / jnp.sqrt(
        jnp.sum(raised * raised, -1, keepdims=True) + 1e-06
    )
    return (raised * rescale).astype(jnp.bfloat16)


def per_device(
    query_feats,
    key_feats,
    value_feats,
    target,
    token_rates,
    row_reach,
    view_counts,
    w_first,
    w_third,
    w_second,
):
    row_count = query_feats.shape[1]
    col_count = query_feats.shape[2]
    feat_width = query_feats.shape[3]
    heads_here = feat_width // HD
    tokens_here = row_count * col_count
    key_span = row_count + 2 * HALO
    grid_rows = lax.axis_size("row") * row_count
    row_base = lax.axis_index("row") * row_count
    view_total = view_counts[0]
    total_valid = lax.psum(view_total.astype(jnp.float32), "view")
    paired = jnp.stack([key_feats[0], value_feats[0]], 0)
    padded = with_halo(paired, (("row", 1),), HALO)
    q_row_ids = row_base + jnp.repeat(jnp.arange(row_count, dtype=jnp.int32), col_count)
    k_row_ids = row_base - HALO + jnp.repeat(jnp.arange(key_span, dtype=jnp.int32), col_count)
    q_tok = q_row_ids * col_count + jnp.tile(jnp.arange(col_count, dtype=jnp.int32), row_count)
    k_tok = k_row_ids * col_count + jnp.tile(jnp.arange(col_count, dtype=jnp.int32), key_span)
    k_valid = k_tok < view_total
    q_reach = jnp.repeat(row_reach, col_count)
    attended = attend(
        query_feats[0].reshape(tokens_here, feat_width),
        padded[0].reshape(key_span * col_count, feat_width),
        padded[1].reshape(key_span * col_count, feat_width),
        q_row_ids,
        k_row_ids,
        q_tok,
        k_tok,
        k_valid,
        q_reach,
        grid_rows,
    )
    attended = attended.reshape(tokens_here, heads_here, HD).astype(jnp.float32)
    fast_keys = (
        attended * lax.rsqrt(jnp.mean(attended * attended, -1, keepdims=True) + 1e-06)
    ).astype(jnp.bfloat16)
    valid_mask = (q_tok < view_total).astype(jnp.float32)
    rates_tok = token_rates[0].T
    scaled = (
        rates_tok[:, :, None]
        * valid_mask[:, None, None]
        * target[0].reshape(tokens_here, heads_here, HD).astype(jnp.float32)
    ).astype(jnp.bfloat16)
    first_proj = jnp.einsum("thi,hij->thj", fast_keys, w_first, preferred_element_type=jnp.float32)
    third_proj = jnp.einsum("thi,hij->thj", fast_keys, w_third, preferred_element_type=jnp.float32)
    gated_rows = (jax.nn.silu(first_proj) * third_proj).astype(jnp.bfloat16)
    back_rows = jnp.einsum("tho,hjo->thj", scaled, w_second, preferred_element_type=jnp.float32)
    back_first = (back_rows * third_proj * silu_slope(first_proj)).astype(jnp.bfloat16)
    back_third = (back_rows * jax.nn.silu(first_proj)).astype(jnp.bfloat16)
    grad_first = jnp.einsum(
        "thi,thj->hij", fast_keys, back_first, preferred_element_type=jnp.float32
    )
    grad_third = jnp.einsum(
        "thi,thj->hij", fast_keys, back_third, preferred_element_type=jnp.float32
    )
    grad_second = jnp.einsum("thj,tho->hjo", gated_rows, scaled, preferred_element_type=jnp.float32)
    grad_first, grad_third, grad_second = lax.psum(
        (grad_first, grad_third, grad_second), ("view", "row")
    )
    new_first = renorm(w_first, grad_first, total_valid)
    new_third = renorm(w_third, grad_third, total_valid)
    new_second = renorm(w_second, grad_second, total_valid)
    applied = (
        jax.nn.silu(
            jnp.einsum("thi,hij->thj", fast_keys, new_first, preferred_element_type=jnp.float32)
        )
        * jnp.einsum("thi,hij->thj", fast_keys, new_third, preferred_element_type=jnp.float32)
    ).astype(jnp.bfloat16)
    fast_out = jnp.einsum(
        "thj,hjo->tho", applied, new_second, preferred_element_type=jnp.float32
    ).astype(jnp.bfloat16)
    return fast_out.reshape(1, row_count, col_count, feat_width)


def halve(values_in, size):
    if size & (size - 1) == 0:
        return values_in >> (size.bit_length() - 1)
    return lax.div(values_in, jnp.int32(size))


def dot(left, right, dims=(((1,), (0,)), ((), ()))):
    return lax.dot_general(left, right, dims, preferred_element_type=F32)


def flip(index, bits):
    bit = 1
    while bit <= bits:
        if bits & bit:
            index = index + bit - 2 * bit * lax.rem(lax.div(index, bit), 2)
        bit *= 2
    return index


def step_kernel(
    nr, nz, cols,
    q_hbm, k_hbm, v_hbm, t_hbm, rates_hbm, reach_hbm, count_hbm, wf_hbm, wt_hbm, ws_hbm,
    out_ref,
    q_ref, k_ref, v_ref, t_ref, rates_ref, reach_ref, count_ref, wf, wt, ws, halo, raw, kall, sall, cnt, gfull, gsend, grecv,
    wtr, news, ss, ssz, osend, orecv, load_sem, send_sem, recv_sem,
):
    tokens, width = q_ref.shape
    rows_here = tokens // cols
    hid = width // nr
    part = hid // nz
    edge = HALO * cols
    heads = width // ATT_HD
    me = lax.axis_index("row")
    mz = lax.axis_index("view")
    mine = pl.ds(pl.multiple_of(me * hid, hid), hid)
    here = pl.ds(pl.multiple_of(mz * part, part), part)

    def view_peer(bits):
        return flip(mz, bits)

    barrier = pltpu.get_barrier_semaphore()
    for d in range(1, nr):
        pl.semaphore_signal(barrier, inc=1, device_id={"row": flip(me, d)}, device_id_type=MESH)
    for d in range(1, nz):
        pl.semaphore_signal(barrier, inc=1, device_id={"view": view_peer(d)}, device_id_type=MESH)
    loads = [
        pltpu.make_async_copy(source, target, load_sem.at[i])
        for i, (source, target) in enumerate((
            (count_hbm, count_ref), (reach_hbm, reach_ref), (k_hbm, k_ref), (v_hbm, v_ref),
            (t_hbm, t_ref), (rates_hbm, rates_ref), (q_hbm, q_ref),
            (wf_hbm.at[:, mine], wf), (wt_hbm.at[:, mine], wt), (ws_hbm.at[mine, :], ws),
        ))
    ]
    for load in loads:
        load.start()

    used = [0]

    def send(source, target, axis, peer):
        slot = used[0]
        used[0] += 1
        copy = pltpu.make_async_remote_copy(
            src_ref=source, dst_ref=target,
            send_sem=send_sem.at[slot], recv_sem=recv_sem.at[slot],
            device_id={axis: peer}, device_id_type=MESH,
        )
        copy.start()
        return copy

    straight = [1] + list(range(2, nr, 2))

    def spread(at):
        return {d: send(at(0), at(d), "row", flip(me, d)) for d in straight}

    def hand_on(at, copies):
        for d in range(2, nr, 2):
            copies[d].wait_recv()
            copies[d + 1] = send(at(d), at(d + 1), "row", flip(me, 1))

    def settle(copies):
        for d in copies:
            copies[d].wait_send()

    above = lax.rem(me + 1, nr)
    below = lax.rem(me + (nr - 1), nr)

    row_base = me * rows_here
    tok_base = me * tokens
    for load in loads[:2]:
        load.wait()
    view_total = count_ref[0]
    cnt[0] = jnp.full((8, 128), view_total, jnp.int32).astype(F32)
    sub = lax.broadcasted_iota(jnp.int32, (tokens, tokens), 0)
    lane = lax.broadcasted_iota(jnp.int32, (tokens, tokens), 1)
    tok_col = tok_base + lax.broadcasted_iota(jnp.int32, (tokens, 1), 0)
    valid_col = (tok_col < view_total).astype(F32)
    for load in loads[2:6]:
        load.wait()
    rate_col = jnp.sum(jnp.where(sub == lane, rates_ref[...], 0.0), axis=1, keepdims=True)
    sall[0] = (rate_col * valid_col * t_ref[...].astype(F32)).astype(BF16)

    def allowed(q_tok, k_tok):
        q_row = halve(q_tok, cols)
        k_row = halve(k_tok + edge, cols) - HALO
        reach = jnp.zeros(q_tok.shape, jnp.int32)
        for r in range(rows_here):
            reach = jnp.where(q_row == r, reach_ref[r], reach)
        k_abs = k_row + row_base
        return (
            (jnp.abs(k_row - q_row) <= reach)
            & (k_abs >= 0)
            & (k_abs < nr * rows_here)
            & ((k_tok + tok_base < view_total) | (k_tok == q_tok))
        )

    near_ok = allowed(sub, lane)
    far_q = lax.broadcasted_iota(jnp.int32, (tokens, 2 * edge), 0)
    far_k = lax.broadcasted_iota(jnp.int32, (tokens, 2 * edge), 1)
    far_ok = allowed(far_q, jnp.where(far_k < edge, far_k - edge, far_k - edge + tokens))
    root = 1.0 / math.sqrt(ATT_HD)
    spans = [slice(h * ATT_HD, (h + 1) * ATT_HD) for h in range(heads)]
    loads[6].wait()
    near = [
        jnp.where(near_ok, dot(q_ref[:, hs], k_ref[:, hs], NT) * root, -1e30) for hs in spans
    ]
    near_top = [jnp.max(scores, axis=-1, keepdims=True) for scores in near]

    pl.semaphore_wait(barrier, (nr - 1) + (nz - 1))

    halo_copies = []
    for i, ref in enumerate((k_ref, v_ref)):
        halo_copies.append(send(ref.at[pl.ds(tokens - edge, edge)], halo.at[i, pl.ds(0, edge)], "row", above))
        halo_copies.append(send(ref.at[pl.ds(0, edge)], halo.at[i, pl.ds(edge, edge)], "row", below))
    s_copies = spread(lambda d: sall.at[d])
    c_copies = [send(cnt.at[0], cnt.at[d], "view", view_peer(d)) for d in range(1, nz)]
    for load in loads[7:]:
        load.wait()
    wtr[0] = wf[...].astype(F32).T
    wtr[1] = wt[...].astype(F32).T
    wtr[2] = ws[...].astype(F32)
    for copy in halo_copies:
        copy.wait()
    k_copies = []
    for h, hs in enumerate(spans):
        far = jnp.where(far_ok, dot(q_ref[:, hs], halo[0, :, hs], NT) * root, -1e30)
        top = jnp.maximum(near_top[h], jnp.max(far, axis=-1, keepdims=True))
        near_pow = jnp.exp(near[h] - top)
        far_pow = jnp.exp(far - top)
        inverse = 1.0 / (
            jnp.sum(near_pow, axis=-1, keepdims=True) + jnp.sum(far_pow, axis=-1, keepdims=True)
        )
        piece = dot((near_pow * inverse).astype(BF16), v_ref[:, hs]) + dot(
            (far_pow * inverse).astype(BF16), halo[1, :, hs]
        )
        raw[0, h] = piece.astype(BF16)
        k_copies.append(spread(lambda d, h=h: raw.at[d, h]))
    hand_on(lambda d: sall.at[d], s_copies)

    def normalise(d):
        pieces = [raw[d, h].astype(F32) for h in range(heads)]
        total_sq = jnp.sum(pieces[0] * pieces[0], axis=-1, keepdims=True)
        for piece in pieces[1:]:
            total_sq = total_sq + jnp.sum(piece * piece, axis=-1, keepdims=True)
        norm = lax.rsqrt(total_sq * (1.0 / width) + 1e-06)
        for hs, piece in zip(spans, pieces):
            kall[d, :, hs] = (piece * norm).astype(BF16)

    def factors(d):
        normalise(d)
        first = dot(kall[d], wf[...])
        third = dot(kall[d], wt[...])
        back = dot(sall[d], ws[...], NT)
        sig = jax.nn.sigmoid(first)
        gate = first * sig
        return (
            ((back * third * (sig * (1.0 + first * (1.0 - sig)))).astype(BF16), kall),
            ((back * gate).astype(BF16), kall),
            ((gate * third).astype(BF16), sall),
        )

    order = [0] + straight + list(range(3, nr, 2))
    g_copies = []
    for d in order:
        if d == 2:
            for h in range(heads):
                hand_on(lambda e, h=h: raw.at[e, h], k_copies[h])
        if d % 2:
            for copies in k_copies + [s_copies]:
                copies[d].wait_recv()
        for m, (left, right) in enumerate(factors(d)):
            grad = dot(left, right[d], TN)
            if d:
                grad = gfull[m] + grad
            gfull[m] = grad
            if d == order[-1]:
                for z in range(nz):
                    gsend[z, m] = grad[z * part:(z + 1) * part].astype(BF16)
                for e in range(nz - 1, 0, -1):
                    g_copies.append(
                        send(gsend.at[view_peer(e), m], grecv.at[e - 1, m], "view", view_peer(e))
                    )
    ss[0, 2:3] = jnp.sum(wtr[0] * wtr[0], axis=0, keepdims=True)
    ss[0, 3:4] = jnp.sum(wtr[1] * wtr[1], axis=0, keepdims=True)
    for copy in c_copies:
        copy.wait()
    total_valid = cnt[0, 0:1, 0:1]
    for d in range(1, nz):
        total_valid = total_valid + cnt[d, 0:1, 0:1]

    w_copies = []
    for m in range(3):
        for copy in g_copies[m * (nz - 1):(m + 1) * (nz - 1)]:
            copy.wait()
        grad = gfull[m, here, :]
        for d in range(1, nz):
            grad = grad + grecv[d - 1, m].astype(F32)
        old = wtr[m, here, :]
        raised = old + grad / total_valid
        if m == 2:
            rescale = jnp.sqrt(jnp.sum(old * old, -1, keepdims=True) + 1e-06) / jnp.sqrt(
                jnp.sum(raised * raised, -1, keepdims=True) + 1e-06
            )
            raised = raised * rescale
        else:
            ss[0, m:m + 1] = jnp.sum(raised * raised, axis=0, keepdims=True)
        news[0, m] = raised.astype(BF16)
        for d in range(nz - 1, 0, -1):
            w_copies.append(send(news.at[0, m], news.at[d, m], "view", view_peer(d)))
        if m == 1:
            ss_copies = [send(ss.at[0], ss.at[d], "row", flip(me, d)) for d in range(1, nr)]
    for copy in ss_copies:
        copy.wait()
    strip_sums = ss[0]
    for d in range(1, nr):
        strip_sums = strip_sums + ss[d]
    ssz[0] = strip_sums[0:2]
    ssz_copies = [send(ssz.at[0], ssz.at[d], "view", view_peer(d)) for d in range(1, nz)]
    for copy in ssz_copies:
        copy.wait()
    new_sums = ssz[0]
    for d in range(1, nz):
        new_sums = new_sums + ssz[d]
    scales = jnp.sqrt(strip_sums[2:4] + 1e-06) / jnp.sqrt(new_sums + 1e-06)

    for copy in w_copies:
        copy.wait()
    new_first, new_third, new_second = (
        jnp.concatenate([news[d, m] for d in range(nz)], axis=0) for m in range(3)
    )

    def share(d):
        keys = kall[d].astype(F32)
        first = dot((keys * scales[0:1]).astype(BF16), new_first, NT)
        third = dot((keys * scales[1:2]).astype(BF16), new_third, NT)
        return dot((first * jax.nn.sigmoid(first) * third).astype(BF16), new_second)

    o_copies = {}
    for d in list(range(3, nr, 2)) + list(range(2, nr, 2)) + [1, 0]:
        total = share(d)
        if d == 0:
            continue
        if d % 2 == 0:
            o_copies[d + 1].wait_recv()
            total = total + orecv[d].astype(F32)
        osend[d - 1] = total.astype(BF16)
        o_copies[d] = send(
            osend.at[d - 1], orecv.at[d - 1], "row", flip(me, 1) if d % 2 else flip(me, d)
        )
    for d in [1] + list(range(2, nr, 2)):
        o_copies[d].wait_recv()
        total = total + orecv[d - 1].astype(F32)
    out_ref[...] = total.astype(BF16)
    for copies in k_copies + [s_copies, o_copies]:
        settle(copies)


def fused_step(
    nr, nz,
    query_feats, key_feats, value_feats, target, token_rates, row_reach, view_counts,
    w_first, w_third, w_second,
):
    _, row_count, cols, width = query_feats.shape
    tokens = row_count * cols
    hid = width // nr
    part = hid // nz
    edge = HALO * cols
    heads = width // ATT_HD
    copies = 4 + (3 + heads) * (nr - 1) + 8 * (nz - 1)
    anywhere = pl.BlockSpec(memory_space=pl.ANY)
    flat = lambda a: a.reshape(tokens, width)
    out = pl.pallas_call(
        functools.partial(step_kernel, nr, nz, cols),
        out_shape=pltpu.VMEM((tokens, width), BF16),
        in_specs=[anywhere] * 5 + [pl.BlockSpec(memory_space=pltpu.HBM)] * 2 + [anywhere] * 3,
        out_specs=pl.BlockSpec(memory_space=pltpu.VMEM),
        scratch_shapes=[
            pltpu.VMEM((tokens, width), BF16),
            pltpu.VMEM((tokens, width), BF16),
            pltpu.VMEM((tokens, width), BF16),
            pltpu.VMEM((tokens, width), BF16),
            pltpu.VMEM((1, tokens), F32),
            pltpu.SMEM((row_count,), jnp.int32),
            pltpu.SMEM((1,), jnp.int32),
            pltpu.VMEM((width, hid), BF16),
            pltpu.VMEM((width, hid), BF16),
            pltpu.VMEM((hid, width), BF16),
            pltpu.VMEM((2, 2 * edge, width), BF16),
            pltpu.VMEM((nr, heads, tokens, ATT_HD), BF16),
            pltpu.VMEM((nr, tokens, width), BF16),
            pltpu.VMEM((nr, tokens, width), BF16),
            pltpu.VMEM((nz, 8, 128), F32),
            pltpu.VMEM((3, hid, width), F32),
            pltpu.VMEM((nz, 3, part, width), BF16),
            pltpu.VMEM((nz - 1, 3, part, width), BF16),
            pltpu.VMEM((3, hid, width), F32),
            pltpu.VMEM((nz, 3, part, width), BF16),
            pltpu.VMEM((nr, 4, width), F32),
            pltpu.VMEM((nz, 2, width), F32),
            pltpu.VMEM((nr - 1, tokens, width), BF16),
            pltpu.VMEM((nr - 1, tokens, width), BF16),
            pltpu.SemaphoreType.DMA((10,)),
            pltpu.SemaphoreType.DMA((copies,)),
            pltpu.SemaphoreType.DMA((copies,)),
        ],
        compiler_params=pltpu.CompilerParams(collective_id=0, has_side_effects=True),
    )(
        flat(query_feats), flat(key_feats), flat(value_feats), flat(target),
        token_rates.reshape(1, tokens), row_reach, view_counts,
        w_first.reshape(width, width), w_third.reshape(width, width), w_second.reshape(width, width),
    )
    return out.reshape(query_feats.shape)


def solution(mesh):
    placed = (
        P("view", "row", None, "head"),
        P("view", "row", None, "head"),
        P("view", "row", None, "head"),
        P("view", "row", None, "head"),
        P("view", "head", "row"),
        P("row"),
        P("view"),
        P("head", None, None),
        P("head", None, None),
        P("head", None, None),
    )
    nr, nz = mesh.shape["row"], mesh.shape["view"]
    pairs = nr > 1 and nr & (nr - 1) == 0
    fits = pairs and nz > 1 and nz & (nz - 1) == 0 and HD % (128 * nr) == 0 and HD % (16 * nr * nz) == 0
    return jax.shard_map(
        functools.partial(fused_step, nr, nz) if fits else per_device,
        mesh=mesh,
        in_specs=placed,
        out_specs=P("view", "row", None, "head"),
        check_vma=False,
    )
```
